32 devices in a mesh: obs: 2 (over x), chan: 8 (over z, y), tm: 2 (over core).
Axes of the slice: x: 2, y: 2, z: 4, core: 2. Of those that a mesh axis runs over, the one named last changes fastest.
Arguments:
- residuals: bfloat16 [16, 4, 2, 1024, 1024], P(('obs', 'chan'), 'tm'), parts along dimension 0, may hold values from -0.125 to 0.125
- flag_masks: int32 [16, 4, 512], P(('obs', 'chan')), parts along dimension 0, may hold values 0 or 1
- cluster: int32 [128], P('obs'), parts along dimension 0, may hold values from 0 to 7
- penalty: float32 [16], P('obs'), parts along dimension 0, may hold values from 0.25 to 4
- jones_init: float32 [16, 1024, 256], P(('obs', 'chan')), parts along dimension 0, may hold values from -6 to 6
- duals_init: float32 [16, 1024, 256], P(('obs', 'chan')), parts along dimension 0, may hold values from -4 to 4
Outputs:
- jones_out: float32 [16, 1024, 256], P(('obs', 'chan'), 'tm'), parts along dimension 0
- duals_out: float32 [16, 1024, 256], P(('obs', 'chan'), 'tm'), parts along dimension 0
The draws below stay inside these ranges and needn't reach their ends.
There are 2 independent parts, one for each index of `obs`. The reference program is written for one: setup_inputs(seed, part) draws one part's arguments, and reference() takes and returns one part's arrays. A program takes and returns all parts, laid end to end along the dimension named above; each array names one. Nothing has to cross between parts.
All inputs are finite; a program needn't handle non-finite values. No bound on the sum of `flag_masks` on one device may be relied on, other than what follows from the above.
Results may differ from the reference program's by a relative error of at most 0.0054.
Values may be sent and summed in bfloat16 or wider, within the bound.
No kernel may reach another device: no remote copies, remote signals or barrier semaphores. Data moves between devices by JAX's collectives and lax.ppermute only.
A program may use at most 64 MiB of HBM per device.

```python
import math
import jax
import jax.numpy as jnp
from jax import lax

STATIONS = 512
ROWS = 1024
DIRS = 64
COLS = 128
CLUSTERS = 8
POLY = 3
ITERS = 2
CHANNELS = 8
SLOTS = 4


def set_ends(entries, rng, low, top_value):
    spot = [jax.random.randint(jax.random.fold_in(rng, axis), (), 0, length) for axis, length in enumerate(entries.shape)]
    longest = entries.shape.index(max(entries.shape))
    neighbour = spot[:longest] + [(spot[longest] + 1) % entries.shape[longest]] + spot[longest + 1:]
    return entries.at[tuple(spot)].set(low).at[tuple(neighbour)].set(top_value)


def block_levels(key, shape, cuts, least, top_value):
    def one(dim, shards_of):
        steps = jax.random.uniform(jax.random.fold_in(jax.random.fold_in(key, 6), dim), (shards_of,), jnp.float32, least / len(cuts), top_value / len(cuts))
        return jnp.repeat(jnp.exp(steps), shape[dim] // shards_of).reshape((-1,) + (1,) * (len(shape) - dim - 1))

    factor_of = one(*cuts[0])
    for cut in cuts[1:]:
        factor_of = factor_of * one(*cut)
    return factor_of


def bell_draw(stream_key, extent, scale, reach, cuts=(), kind=jnp.bfloat16):
    level = block_levels(stream_key, extent, cuts, -0.22, 0.18) if cuts else 1.0
    result = jax.random.normal(stream_key, extent, jnp.float32) * scale * level
    return jnp.minimum(jnp.maximum(result, -reach), reach).astype(kind)


def setup_inputs(seed: int = 0, part: int = 0) -> dict:
    arg_keys = jax.random.split(jax.random.key(seed), 7)
    part_splits = jax.random.split(jax.random.fold_in(arg_keys[6], part), 7)
    return {
        "residuals": bell_draw(part_splits[0], (CHANNELS, SLOTS, 2, ROWS, ROWS), (2 * ROWS) ** -0.5, 0.125, ((0, 8), (1, 2))),
        "flag_masks": set_ends((jax.random.randint(part_splits[1], (CHANNELS, SLOTS, STATIONS), 0, 4) < 3).astype(jnp.int32), jax.random.fold_in(part_splits[1], 1), 0, 1),
        "cluster": set_ends(jax.random.randint(part_splits[2], (DIRS,), 0, CLUSTERS), jax.random.fold_in(part_splits[2], 1), 0, CLUSTERS - 1).astype(jnp.int32),
        "penalty": jnp.clip(jnp.exp(jax.random.uniform(part_splits[3], (CLUSTERS,), jnp.float32, math.log(0.25), math.log(4.0))), 0.25, 4.0),
        "jones_init": bell_draw(part_splits[4], (CHANNELS, ROWS, 2 * COLS), 1.0, 6.0, ((0, 8),), jnp.float32),
        "duals_init": bell_draw(part_splits[5], (CHANNELS, ROWS, 2 * COLS), 0.5, 4.0, ((0, 8),), jnp.float32),
    }


def poly_basis(total_count):
    position = (2.0 * jnp.arange(total_count, dtype=jnp.float32) + 1.0) / total_count - 1.0
    columns = []
    for degree in range(POLY):
        column = position ** degree
        for previous in columns:
            column = column - jnp.sum(column * previous) * previous
        column = column / jnp.sqrt(jnp.sum(column * column))
        columns.append(column)
    return jnp.stack(columns, axis=1)

def column_rates(cluster, penalty):
    labels = jnp.arange(penalty.shape[0], dtype=jnp.int32)
    onehot = (cluster[:, None] == labels[None, :]).astype(jnp.float32)
    per_dir = lax.optimization_barrier(jnp.sum(onehot * penalty[None, :], axis=1))
    per_col = jnp.repeat(per_dir, 2)
    return jnp.concatenate([per_col, per_col])

def complex_apply(resid_re, resid_im, operand, half_cols):
    real_part = jnp.dot(resid_re, operand, preferred_element_type=jnp.float32)
    imag_part = jnp.dot(resid_im, operand, preferred_element_type=jnp.float32)
    return jnp.concatenate([real_part[:, :half_cols] - imag_part[:, half_cols:], real_part[:, half_cols:] + imag_part[:, :half_cols]], axis=1)

def admm_update(gradient, target, dual_vars, counts, col_rates):
    return (gradient + col_rates * (target - dual_vars)) / (counts[:, :, None] + col_rates)

def channel_gradient(entry):
    resid_chan, flag_chan, jones_chan = entry
    rounded = jones_chan.astype(jnp.bfloat16)
    half_cols = jones_chan.shape[1] // 2

    def add_slot(running, slot_entry):
        resid, flag_row = slot_entry
        row_mask = jnp.repeat(flag_row.astype(jnp.float32), 2)
        operand = row_mask.astype(jnp.bfloat16)[:, None] * rounded
        product = complex_apply(resid[0], resid[1], operand, half_cols)
        return (running + row_mask[:, None] * product, None)
    start_sum = jnp.zeros(jones_chan.shape, jnp.float32)
    running, _ = lax.scan(add_slot, start_sum, (resid_chan, flag_chan))
    return running

def reference(residuals, flag_masks, cluster, penalty, jones_init, duals_init):
    basis = poly_basis(residuals.shape[0])
    col_rates = column_rates(cluster, penalty)
    counts = jnp.repeat(lax.optimization_barrier(jnp.sum(flag_masks.astype(jnp.float32), axis=1)), 2, axis=1)
    jones_now = jones_init
    dual_vars = duals_init
    target = jones_init
    for sweep in range(ITERS):
        gradient = lax.map(channel_gradient, (residuals, flag_masks, jones_now))
        jones_now = admm_update(gradient, target, dual_vars, counts, col_rates)
        coeffs = jnp.einsum('fp,frc->prc', basis, jones_now + dual_vars, precision=lax.Precision.HIGHEST)
        target = jnp.einsum('fp,prc->frc', basis, coeffs, precision=lax.Precision.HIGHEST)
        dual_vars = dual_vars + jones_now - target
    return (jones_now, dual_vars)
```

```python
import functools

import jax
import jax.numpy as jnp
import numpy as np
from jax import lax
from jax.experimental import pallas as pl
from jax.experimental.pallas import tpu as pltpu
from jax.sharding import PartitionSpec as P

POLY = 3
WIRE = jnp.bfloat16
F32 = jnp.float32
LANES = 128
TILE = 16
MIB = 1 << 20


def poly_basis(total_count):
    position = (2.0 * np.arange(total_count) + 1.0) / total_count - 1.0
    columns = []
    for degree in range(POLY):
        column = position**degree
        for previous in columns:
            column = column - np.sum(column * previous) * previous
        columns.append(column / np.sqrt(np.sum(column * column)))
    return np.stack(columns, axis=1).astype(np.float32)


def eye_mask(rows):
    shape = (rows, max(rows, LANES))
    return lax.broadcasted_iota(jnp.int32, shape, 0) == lax.broadcasted_iota(jnp.int32, shape, 1)


def column_of(table, lane):
    lanes = lax.broadcasted_iota(jnp.int32, table.shape, 1)
    return jnp.sum(jnp.where(lanes == lane, table, 0.0), axis=1, keepdims=True)


def fill_operands(xs_ref, rounded, mask_col):
    half = rounded.shape[1] // 2
    masked = mask_col.astype(jnp.bfloat16) * rounded
    xs_ref[0] = masked
    xs_ref[1] = jnp.concatenate([-masked[:, half:], masked[:, :half]], axis=1)


def first_kernel(
    tm_ref, resid_ref, flags_ref, cluster_ref, penalty_ref, jones_ref, duals_ref,
    grad_ref, table_ref, rates_ref, xs_ref, acc_ref,
):
    slot, plane = pl.program_id(0), pl.program_id(1)
    slots_here = pl.num_programs(0)
    rows, cols = jones_ref.shape
    slots = flags_ref.shape[0]
    share = pl.num_programs(0)

    @pl.when((slot == 0) & (plane == 0))
    def _():
        flags = flags_ref[...].astype(F32)
        stations = flags.shape[1]
        total = jnp.sum(flags, axis=0, keepdims=True)
        row_id = lax.broadcasted_iota(jnp.int32, (LANES, stations), 0)
        stacked = jnp.zeros((LANES, stations), F32)
        for t in range(slots):
            stacked = jnp.where(row_id == t, flags[t : t + 1], stacked)
        stacked = jnp.where(row_id == slots, total, stacked)
        pick = (
            lax.broadcasted_iota(jnp.int32, (rows, stations), 0) // 2
            == lax.broadcasted_iota(jnp.int32, (rows, stations), 1)
        )
        table_ref[...] = lax.dot_general(
            pick.astype(jnp.bfloat16), stacked.astype(jnp.bfloat16),
            (((1,), (1,)), ((), ())), preferred_element_type=F32,
        )
        dirs = cluster_ref.shape[1]
        lane = lax.broadcasted_iota(jnp.int32, (dirs, cols), 1)
        spread = lax.rem(lane, cols // 2) // 2 == lax.broadcasted_iota(jnp.int32, (dirs, cols), 0)
        labels = jnp.broadcast_to(cluster_ref[...].astype(F32), (8, dirs)).astype(jnp.bfloat16)
        label = jnp.dot(labels, spread.astype(jnp.bfloat16), preferred_element_type=F32)
        rates = jnp.zeros((8, cols), F32)
        for k in range(penalty_ref.shape[0]):
            rates = jnp.where(label == k, penalty_ref[k], rates)
        rates_ref[...] = rates

    mask_col = column_of(table_ref[...], tm_ref[0] * share + slot)

    @pl.when(plane == 0)
    def _():
        fill_operands(xs_ref, jones_ref[...].astype(jnp.bfloat16), mask_col)
        acc_ref[...] = jnp.dot(resid_ref[...], xs_ref[0], preferred_element_type=F32)

    @pl.when(plane == 1)
    def _():
        product = acc_ref[...] + jnp.dot(resid_ref[...], xs_ref[1], preferred_element_type=F32)

        @pl.when(slot == 0)
        def _():
            half_term = (1.0 / tm_ref[1].astype(F32)) * rates_ref[0:1] * (jones_ref[...] - duals_ref[...])
            grad_ref[...] = half_term + mask_col * product

        @pl.when(slot > 0)
        def _():
            grad_ref[...] = grad_ref[...] + mask_col * product


def second_kernel(
    tm_ref, resid_ref, mine_ref, theirs_ref, table_ref, rates_ref, duals_ref,
    u_ref, own_ref, other_ref, x_ref, xs_ref, acc_ref, sum_ref,
):
    slot, plane = pl.program_id(0), pl.program_id(1)
    share = pl.num_programs(0)
    slots = share * 2
    own_rows = u_ref.shape[0]

    @pl.when((slot == 0) & (plane == 0))
    def _():
        counts = column_of(table_ref[...], tm_ref[2])
        acc_ref[...] = (mine_ref[...] + theirs_ref[...]) / (counts + rates_ref[0:1])
        x_ref[...] = acc_ref[...].astype(jnp.bfloat16)
        start = pl.multiple_of(tm_ref[0] * own_rows, own_rows)
        u_ref[...] = acc_ref[pl.ds(start, own_rows), :] + duals_ref[...]

    mask_col = column_of(table_ref[...], tm_ref[0] * share + slot)

    @pl.when(plane == 0)
    def _():
        fill_operands(xs_ref, x_ref[...], mask_col)
        acc_ref[...] = jnp.dot(resid_ref[...], xs_ref[0], preferred_element_type=F32)

    @pl.when(plane == 1)
    def _():
        product = acc_ref[...] + jnp.dot(resid_ref[...], xs_ref[1], preferred_element_type=F32)

        @pl.when(slot == 0)
        def _():
            sum_ref[...] = mask_col * product

        @pl.when(slot > 0)
        def _():
            sum_ref[...] = sum_ref[...] + mask_col * product

        @pl.when(slot == share - 1)
        def _():
            start = pl.multiple_of(tm_ref[0] * own_rows, own_rows)
            away = pl.multiple_of((1 - tm_ref[0]) * own_rows, own_rows)
            own_ref[...] = sum_ref[pl.ds(start, own_rows), :]
            other_ref[...] = sum_ref[pl.ds(away, own_rows), :]


def pack_kernel(members, at_ref, own_ref, theirs_ref, u_ref, table_ref, rates_ref, q_ref, *message_refs):
    rates = rates_ref[0:1]
    counts = column_of(table_ref[...], at_ref[2])
    q_ref[...] = (own_ref[...] + theirs_ref[...] - rates * u_ref[...]) / (counts + rates)
    block = u_ref.shape[0] // members
    eye = eye_mask(block)
    for s, message in enumerate(message_refs):
        rows = pl.ds(pl.multiple_of((at_ref[1] ^ s) * block, block), block)
        message[0:block] = u_ref[rows, :].astype(WIRE)
        message[block : 2 * block] = q_ref[rows, :].astype(WIRE)
        column = column_of(table_ref[rows, :], at_ref[2])
        line = jnp.sum(jnp.where(eye, column, 0.0), axis=0, keepdims=True)
        message[2 * block : 2 * block + TILE, 0 : line.shape[1]] = jnp.broadcast_to(
            line, (TILE, line.shape[1])
        ).astype(WIRE)


def owner_kernel(members, block, at_ref, basis_ref, rates_ref, *refs):
    received, returned = refs[:members], refs[members:]
    rates = rates_ref[0:1]
    eye = eye_mask(block)
    lines = eye.shape[1]
    weights = [[basis_ref[at_ref[1] ^ s, p] for p in range(POLY)] for s in range(members)]
    coeffs = [None] * POLY
    sums = [None] * POLY
    plus = lambda a, b: b if a is None else a + b
    for s in range(members):
        u = received[s][0:block].astype(F32)
        w = u + received[s][block : 2 * block].astype(F32)
        for p in range(POLY):
            coeffs[p] = plus(coeffs[p], weights[s][p] * u)
            sums[p] = plus(sums[p], weights[s][p] * w)
    for s in range(members):
        line = received[s][2 * block : 2 * block + TILE, 0:lines].astype(F32)[0:1]
        counts = jnp.sum(jnp.where(eye, line, 0.0), axis=1, keepdims=True)
        first = weights[s][0] * coeffs[0]
        for p in range(1, POLY):
            first = first + weights[s][p] * coeffs[p]
        returned[s][0:block] = first.astype(WIRE)
        step = (2.0 * rates / (counts + rates)) * first
        for p in range(POLY):
            sums[p] = sums[p] + weights[s][p] * step
    for s in range(members):
        second = weights[s][0] * sums[0]
        for p in range(1, POLY):
            second = second + weights[s][p] * sums[p]
        returned[s][block : 2 * block] = second.astype(WIRE)


def finish_kernel(members, at_ref, q_ref, u_ref, table_ref, rates_ref, *refs):
    received, jones_ref, duals_ref = refs[:members], refs[members], refs[members + 1]
    rates = rates_ref[0:1]
    block = u_ref.shape[0] // members
    for s in range(members):
        rows = pl.ds(pl.multiple_of((at_ref[1] ^ s) * block, block), block)
        counts = column_of(table_ref[rows, :], at_ref[2])
        first = received[s][0:block].astype(F32)
        jones = q_ref[rows, :] + (2.0 * rates / (counts + rates)) * first
        jones_ref[rows, :] = jones
        duals_ref[rows, :] = u_ref[rows, :] + jones - received[s][block : 2 * block].astype(F32)


def vmem(shape, dtype=F32):
    return jax.ShapeDtypeStruct(shape, dtype)


def whole(memory_space=pltpu.VMEM):
    return pl.BlockSpec(memory_space=memory_space)


def params(mib):
    return pltpu.CompilerParams(vmem_limit_bytes=mib * MIB)


def on_device(residuals, flag_masks, cluster, penalty, jones_init, duals_init):
    members, halves = lax.axis_size("chan"), lax.axis_size("tm")
    share, rows = residuals.shape[1], residuals.shape[3]
    slots, cols = flag_masks.shape[1], jones_init.shape[2]
    own_rows = rows // halves
    block = own_rows // members
    chan, tm = lax.axis_index("chan"), lax.axis_index("tm")
    here = jnp.stack([tm, jnp.int32(halves)]).astype(jnp.int32)
    at = jnp.stack([tm, chan, jnp.int32(slots)]).astype(jnp.int32)
    resid = residuals[0]
    jones0, duals0 = jones_init[0], duals_init[0]

    resid_spec = pl.BlockSpec((None, None, rows, rows), lambda t, p, *_: (t, p, 0, 0))
    full = lambda shape: pl.BlockSpec(shape, lambda t, p, *_: (0,) * len(shape))
    grad, table, rates = pl.pallas_call(
        first_kernel,
        out_shape=(vmem((rows, cols)), vmem((rows, LANES)), vmem((8, cols))),
        grid_spec=pltpu.PrefetchScalarGridSpec(
            num_scalar_prefetch=1,
            grid=(share, 2),
            in_specs=[
                resid_spec, full((slots, rows // 2)), full((1, cluster.shape[0])),
                pl.BlockSpec(memory_space=pltpu.SMEM), full((rows, cols)), full((rows, cols)),
            ],
            out_specs=[full((rows, cols)), full((rows, LANES)), full((8, cols))],
            scratch_shapes=[pltpu.VMEM((2, rows, cols), jnp.bfloat16), pltpu.VMEM((rows, cols), F32)],
        ),
        compiler_params=params(30),
        name="first",
    )(here, resid, flag_masks[0], cluster[None, :], penalty, jones0, duals0)

    swap = [(0, 1), (1, 0)]
    grad_other = lax.ppermute(grad, "tm", swap)

    u, own, other = pl.pallas_call(
        second_kernel,
        out_shape=(vmem((own_rows, cols)),) * 3,
        grid_spec=pltpu.PrefetchScalarGridSpec(
            num_scalar_prefetch=1,
            grid=(share, 2),
            in_specs=[
                resid_spec, full((rows, cols)), full((rows, cols)), full((rows, LANES)), full((8, cols)),
                pl.BlockSpec((own_rows, cols), lambda t, p, at_ref: (at_ref[0], 0)),
            ],
            out_specs=[full((own_rows, cols))] * 3,
            scratch_shapes=[
                pltpu.VMEM((rows, cols), jnp.bfloat16), pltpu.VMEM((2, rows, cols), jnp.bfloat16),
                pltpu.VMEM((rows, cols), F32), pltpu.VMEM((rows, cols), F32),
            ],
        ),
        compiler_params=params(30),
        name="second",
    )(at, resid, grad, grad_other, table, rates, duals0)
    theirs = lax.ppermute(other, "tm", swap)

    own_table = lax.dynamic_slice_in_dim(table, tm * own_rows, own_rows, 0)
    smem = whole(pltpu.SMEM)
    q, *messages = pl.pallas_call(
        functools.partial(pack_kernel, members),
        out_shape=(vmem((own_rows, cols)),) + (vmem((2 * block + TILE, cols), WIRE),) * members,
        in_specs=[smem] + [whole()] * 5,
        out_specs=[whole()] * (1 + members),
        compiler_params=params(16),
        name="pack",
    )(at, own, theirs, u, own_table, rates)

    def exchange(parts):
        got = [None] * members
        got[0] = parts[0]
        for s in sorted(range(1, members), reverse=True):
            got[s] = lax.ppermute(parts[s], "chan", [(f, f ^ s) for f in range(members)])
        return got

    messages = exchange(messages)
    returned = pl.pallas_call(
        functools.partial(owner_kernel, members, block),
        out_shape=(vmem((2 * block, cols), WIRE),) * members,
        in_specs=[smem, smem] + [whole()] * (1 + members),
        out_specs=[whole()] * members,
        compiler_params=params(16),
        name="owner",
    )(at, jnp.asarray(poly_basis(members)), rates, *messages)
    returned = exchange(returned)
    jones, duals = pl.pallas_call(
        functools.partial(finish_kernel, members),
        out_shape=(vmem((own_rows, cols)),) * 2,
        in_specs=[smem] + [whole()] * (4 + members),
        out_specs=[whole()] * 2,
        compiler_params=params(16),
        name="finish",
    )(at, q, u, own_table, rates, *returned)
    return jones[None], duals[None]


def solution(mesh):
    in_specs = (
        P(("obs", "chan"), "tm", None, None, None),
        P(("obs", "chan"), None, None),
        P("obs"),
        P("obs"),
        P(("obs", "chan"), None, None),
        P(("obs", "chan"), None, None),
    )
    out_specs = (P(("obs", "chan"), "tm", None), P(("obs", "chan"), "tm", None))
    return jax.shard_map(
        on_device, mesh=mesh, in_specs=in_specs, out_specs=out_specs, check_vma=False
    )
```

```python
import functools

import jax
import jax.numpy as jnp
import numpy as np
from jax import lax
from jax.experimental import pallas as pl
from jax.experimental.pallas import tpu as pltpu
from jax.sharding import PartitionSpec as P

POLY = 3
WIRE = jnp.bfloat16
F32 = jnp.float32
LANES = 128
TILE = 8
MIB = 1 << 20


def poly_basis(total_count):
    position = (2.0 * np.arange(total_count) + 1.0) / total_count - 1.0
    columns = []
    for degree in range(POLY):
        column = position**degree
        for previous in columns:
            column = column - np.sum(column * previous) * previous
        columns.append(column / np.sqrt(np.sum(column * column)))
    return np.stack(columns, axis=1).astype(np.float32)


def eye_mask(rows):
    shape = (rows, max(rows, LANES))
    return lax.broadcasted_iota(jnp.int32, shape, 0) == lax.broadcasted_iota(jnp.int32, shape, 1)


def column_of(table, lane):
    lanes = lax.broadcasted_iota(jnp.int32, table.shape, 1)
    return jnp.sum(jnp.where(lanes == lane, table, 0.0), axis=1, keepdims=True)


def twice(half):
    return jnp.concatenate([half, half], axis=1)


def fill_operands(xs_ref, slot, rounded, mask):
    half = rounded.shape[1] // 2
    masked = mask.astype(jnp.bfloat16) * rounded
    xs_ref[2 * slot] = masked
    xs_ref[2 * slot + 1] = jnp.concatenate([-masked[:, half:], masked[:, :half]], axis=1)


def gradient_rows(resid_ref, xs_ref, mask_ref, rows):
    total = None
    for t in range(resid_ref.shape[0]):
        product = jnp.dot(resid_ref[t, 0, rows, :], xs_ref[2 * t], preferred_element_type=F32)
        product += jnp.dot(resid_ref[t, 1, rows, :], xs_ref[2 * t + 1], preferred_element_type=F32)
        part = twice(mask_ref[t, rows, :]) * product
        total = part if total is None else total + part
    return total


def first_kernel(
    chunks, at_ref, resid_hbm, flags_hbm, cluster_hbm, penalty_hbm, jones_hbm, duals_hbm,
    resid_ref, grad_ref, mask_ref, counts_ref, inverse_ref, rates_ref, duals_ref,
    flags_ref, cluster_ref, penalty_ref, jones_ref, xs_ref, sems,
):
    rows, cols = jones_ref.shape
    slots, stations = flags_ref.shape
    share = resid_ref.shape[0]
    step = rows // chunks
    pieces = [
        (flags_hbm, flags_ref), (cluster_hbm, cluster_ref), (penalty_hbm, penalty_ref), (jones_hbm, jones_ref),
    ]
    for m in range(chunks):
        cut = pl.ds(m * step, step)
        pieces.append((resid_hbm.at[:, :, cut, :], resid_ref.at[:, :, cut, :]))
    pieces.insert(5, (duals_hbm, duals_ref))
    copies = [pltpu.make_async_copy(src, dst, sems.at[k]) for k, (src, dst) in enumerate(pieces)]
    for copy in copies:
        copy.start()

    for copy in copies[:3]:
        copy.wait()
    flags = flags_ref[...].astype(F32)
    pick = (
        lax.broadcasted_iota(jnp.int32, (rows, stations), 0) // 2
        == lax.broadcasted_iota(jnp.int32, (rows, stations), 1)
    ).astype(jnp.bfloat16)

    def rows_of(line):
        spread = jnp.broadcast_to(line, (LANES, stations)).astype(jnp.bfloat16)
        return lax.dot_general(pick, spread, (((1,), (1,)), ((), ())), preferred_element_type=F32)

    for t in range(share):
        line = flags_ref[pl.ds(at_ref[0] * share + t, 1), :].astype(F32)
        mask_ref[t] = rows_of(line)
    counts_ref[...] = rows_of(jnp.sum(flags, axis=0, keepdims=True))
    dirs = cluster_ref.shape[1]
    lane = lax.broadcasted_iota(jnp.int32, (dirs, cols), 1)
    spread = lax.rem(lane, cols // 2) // 2 == lax.broadcasted_iota(jnp.int32, (dirs, cols), 0)
    labels = jnp.broadcast_to(cluster_ref[...].astype(F32), (8, dirs)).astype(jnp.bfloat16)
    label = jnp.dot(labels, spread.astype(jnp.bfloat16), preferred_element_type=F32)
    rates = jnp.zeros((8, cols), F32)
    for k in range(penalty_ref.shape[1]):
        rates = jnp.where(label == k, penalty_ref[0:1, k : k + 1], rates)
    rates_ref[...] = rates
    inverse_ref[...] = 1.0 / (twice(counts_ref[...]) + rates[0:1])

    copies[3].wait()
    rounded = jones_ref[...].astype(jnp.bfloat16)
    for t in range(share):
        fill_operands(xs_ref, t, rounded, twice(mask_ref[t]))
    part = rates[0:1] * (1.0 / at_ref[2].astype(F32))
    for m in range(chunks):
        cut = pl.ds(m * step, step)
        copies[4 if m == 0 else 5 + m].wait()
        total = gradient_rows(resid_ref, xs_ref, mask_ref, cut)
        if m == 0:
            copies[5].wait()
        grad_ref[cut, :] = total + part * (jones_ref[cut, :] - duals_ref[cut, :])


def half_start(index, rows):
    return pl.multiple_of(index * rows, rows)


def other_kernel(
    chunks, at_ref, resid_ref, mine_ref, theirs_ref, mask_ref, inverse_ref, duals_ref,
    u_ref, other_ref, xs_ref,
):
    own_rows = u_ref.shape[0]
    jones = (mine_ref[...] + theirs_ref[...]) * inverse_ref[...]
    rounded = jones.astype(jnp.bfloat16)
    for t in range(resid_ref.shape[0]):
        fill_operands(xs_ref, t, rounded, twice(mask_ref[t]))
    own = pl.ds(half_start(at_ref[0], own_rows), own_rows)
    u_ref[...] = (mine_ref[own, :] + theirs_ref[own, :]) * inverse_ref[own, :] + duals_ref[own, :]
    step = own_rows // chunks
    for m in range(chunks):
        start = half_start(1 - at_ref[0], own_rows) + m * step
        other_ref[m * step : (m + 1) * step] = gradient_rows(
            resid_ref, xs_ref, mask_ref, pl.ds(pl.multiple_of(start, step), step)
        )


def own_kernel(chunks, at_ref, resid_ref, xs_ref, mask_ref, own_ref):
    own_rows = own_ref.shape[0]
    step = own_rows // chunks
    for m in range(chunks):
        start = half_start(at_ref[0], own_rows) + m * step
        own_ref[m * step : (m + 1) * step] = gradient_rows(
            resid_ref, xs_ref, mask_ref, pl.ds(pl.multiple_of(start, step), step)
        )


def pack_kernel(members, at_ref, own_ref, theirs_ref, u_ref, inverse_ref, counts_ref, rates_ref, q_ref, *message_refs):
    rates = rates_ref[0:1]
    own_rows = u_ref.shape[0]
    base = half_start(at_ref[0], own_rows)
    q_ref[...] = (own_ref[...] + theirs_ref[...] - rates * u_ref[...]) * inverse_ref[pl.ds(base, own_rows), :]
    block = own_rows // members
    eye = eye_mask(block)
    for s, message in enumerate(message_refs):
        offset = pl.multiple_of((at_ref[1] ^ s) * block, block)
        rows = pl.ds(offset, block)
        message[0:block] = u_ref[rows, :].astype(WIRE)
        message[block : 2 * block] = q_ref[rows, :].astype(WIRE)
        counts = counts_ref[pl.ds(pl.multiple_of(base + offset, block), block), :]
        line = jnp.sum(jnp.where(eye, counts, 0.0), axis=0, keepdims=True)
        message[2 * block : 2 * block + TILE, 0:LANES] = jnp.broadcast_to(line, (TILE, LANES)).astype(WIRE)


def owner_kernel(members, block, at_ref, basis_ref, rates_ref, *refs):
    received, returned = refs[:members], refs[members:]
    rates = rates_ref[0:1]
    eye = eye_mask(block)
    weights = [[basis_ref[at_ref[1] ^ s, p] for p in range(POLY)] for s in range(members)]
    coeffs = [None] * POLY
    sums = [None] * POLY
    plus = lambda a, b: b if a is None else a + b
    for s in range(members):
        u = received[s][0:block].astype(F32)
        w = u + received[s][block : 2 * block].astype(F32)
        for p in range(POLY):
            coeffs[p] = plus(coeffs[p], weights[s][p] * u)
            sums[p] = plus(sums[p], weights[s][p] * w)
    for s in range(members):
        line = received[s][2 * block : 2 * block + TILE, 0:LANES].astype(F32)[0:1]
        counts = jnp.sum(jnp.where(eye, line, 0.0), axis=1, keepdims=True)
        first = weights[s][0] * coeffs[0]
        for p in range(1, POLY):
            first = first + weights[s][p] * coeffs[p]
        returned[s][0:block] = first.astype(WIRE)
        step = (2.0 * rates / (counts + rates)) * first
        for p in range(POLY):
            sums[p] = sums[p] + weights[s][p] * step
    for s in range(members):
        second = weights[s][0] * sums[0]
        for p in range(1, POLY):
            second = second + weights[s][p] * sums[p]
        returned[s][block : 2 * block] = second.astype(WIRE)


def finish_kernel(members, at_ref, q_ref, u_ref, inverse_ref, rates_ref, *refs):
    received, jones_ref, duals_ref = refs[:members], refs[members], refs[members + 1]
    rates = 2.0 * rates_ref[0:1]
    own_rows = u_ref.shape[0]
    block = own_rows // members
    base = half_start(at_ref[0], own_rows)
    for s in range(members):
        offset = pl.multiple_of((at_ref[1] ^ s) * block, block)
        rows = pl.ds(offset, block)
        inverse = inverse_ref[pl.ds(pl.multiple_of(base + offset, block), block), :]
        jones = q_ref[rows, :] + rates * inverse * received[s][0:block].astype(F32)
        jones_ref[rows, :] = jones
        duals_ref[rows, :] = u_ref[rows, :] + jones - received[s][block : 2 * block].astype(F32)


def shape_of(shape, dtype=F32):
    return jax.ShapeDtypeStruct(shape, dtype)


def in_vmem(shape, dtype=F32):
    return pltpu.VMEM(shape, dtype)


def call(kernel, name, outs, ins, limit, scratch=()):
    return pl.pallas_call(
        kernel, out_shape=tuple(outs), in_specs=[pl.BlockSpec(memory_space=space) for space in ins],
        out_specs=tuple(pl.BlockSpec(memory_space=pltpu.VMEM) for _ in outs), scratch_shapes=scratch,
        compiler_params=pltpu.CompilerParams(vmem_limit_bytes=limit * MIB), name=name,
    )


CHUNKS = 4


def on_device(residuals, flag_masks, cluster, penalty, jones_init, duals_init):
    members, halves = lax.axis_size("chan"), lax.axis_size("tm")
    share, rows = residuals.shape[1], residuals.shape[3]
    slots, cols = flag_masks.shape[1], jones_init.shape[2]
    own_rows = rows // halves
    block = own_rows // members
    at = jnp.stack([lax.axis_index("tm"), lax.axis_index("chan"), jnp.int32(halves)]).astype(jnp.int32)
    smem, vmem, hbm = pltpu.SMEM, pltpu.VMEM, pltpu.HBM
    bf16 = jnp.bfloat16

    resid, grad, masks, counts, inverse, rates, duals0 = call(
        functools.partial(first_kernel, CHUNKS), "first",
        [
            in_vmem(residuals.shape[1:], bf16), in_vmem((rows, cols)), in_vmem((share, rows, LANES)),
            in_vmem((rows, LANES)), in_vmem((rows, cols)), in_vmem((8, cols)), in_vmem((rows, cols)),
        ],
        [smem] + [hbm] * 6, 40,
        [
            vmem((slots, rows // 2), jnp.int32), vmem((1, cluster.shape[0]), jnp.int32),
            vmem((1, penalty.shape[0]), F32), vmem((rows, cols), F32), vmem((2 * share, rows, cols), bf16),
            pltpu.SemaphoreType.DMA((5 + CHUNKS,)),
        ],
    )(at, *(
        pltpu.with_memory_space_constraint(x, hbm)
        for x in (residuals[0], flag_masks[0], cluster[None, :], penalty[None, :], jones_init[0], duals_init[0])
    ))

    swap = [(0, 1), (1, 0)]
    grad_other = lax.ppermute(grad, "tm", swap)
    u, other, xs = call(
        functools.partial(other_kernel, CHUNKS // 2), "other",
        [in_vmem((own_rows, cols)), in_vmem((own_rows, cols)), in_vmem((2 * share, rows, cols), bf16)],
        [smem] + [vmem] * 6, 24,
    )(at, resid, grad, grad_other, masks, inverse, duals0)
    theirs = lax.ppermute(other, "tm", swap)
    (own,) = call(
        functools.partial(own_kernel, CHUNKS // 2), "own", [shape_of((own_rows, cols))], [smem] + [vmem] * 3, 24
    )(at, resid, xs, masks)

    q, *messages = call(
        functools.partial(pack_kernel, members), "pack",
        [shape_of((own_rows, cols))] + [shape_of((2 * block + TILE, cols), WIRE)] * members,
        [smem] + [vmem] * 6, 16,
    )(at, own, theirs, u, inverse, counts, rates)

    def exchange(parts):
        got = [None] * members
        got[0] = parts[0]
        for s in sorted(range(1, members), reverse=True):
            got[s] = lax.ppermute(parts[s], "chan", [(f, f ^ s) for f in range(members)])
        return got

    messages = exchange(messages)
    returned = call(
        functools.partial(owner_kernel, members, block), "owner",
        [shape_of((2 * block, cols), WIRE)] * members, [smem, smem] + [vmem] * (1 + members), 16,
    )(at, jnp.asarray(poly_basis(members)), rates, *messages)
    returned = exchange(returned)
    jones, duals = call(
        functools.partial(finish_kernel, members), "finish",
        [shape_of((own_rows, cols))] * 2, [smem] + [vmem] * (4 + members), 16,
    )(at, q, u, inverse, rates, *returned)
    return jones[None], duals[None]


def solution(mesh):
    in_specs = (
        P(("obs", "chan"), "tm", None, None, None),
        P(("obs", "chan"), None, None),
        P("obs"),
        P("obs"),
        P(("obs", "chan"), None, None),
        P(("obs", "chan"), None, None),
    )
    out_specs = (P(("obs", "chan"), "tm", None), P(("obs", "chan"), "tm", None))
    return jax.shard_map(
        on_device, mesh=mesh, in_specs=in_specs, out_specs=out_specs, check_vma=False
    )
```

```python
import functools

import jax
import jax.numpy as jnp
import numpy as np
from jax import lax
from jax.experimental import pallas as pl
from jax.experimental.pallas import tpu as pltpu
from jax.sharding import PartitionSpec as P


POLY = 3
WIRE = jnp.bfloat16
F32 = jnp.float32
LANES = 128
TILE = 8
MIB = 1 << 20


def poly_basis(total_count):
    position = (2.0 * np.arange(total_count) + 1.0) / total_count - 1.0
    powers = np.stack([position**degree for degree in range(POLY)], axis=1)
    columns = []
    for degree in range(POLY):
        column = np.eye(POLY)[degree]
        for previous in columns:
            column = column - np.sum((powers @ column) * (powers @ previous)) * previous
        columns.append(column / np.sqrt(np.sum((powers @ column) ** 2)))
    return columns


def basis_at(channel, total_count):
    position = (2.0 * channel.astype(F32) + 1.0) * (1.0 / total_count) - 1.0
    values = []
    for column in poly_basis(total_count):
        value = jnp.float32(column[POLY - 1])
        for coefficient in column[POLY - 2 :: -1]:
            value = value * position + np.float32(coefficient)
        values.append(value)
    return values


def eye_mask(rows):
    shape = (rows, max(rows, LANES))
    return lax.broadcasted_iota(jnp.int32, shape, 0) == lax.broadcasted_iota(jnp.int32, shape, 1)


def twice(half):
    return jnp.concatenate([half, half], axis=1)


def fill_operands(xs_ref, slot, rounded, mask):
    half = rounded.shape[1] // 2
    masked = mask.astype(jnp.bfloat16) * rounded
    xs_ref[2 * slot] = masked
    xs_ref[2 * slot + 1] = jnp.concatenate([-masked[:, half:], masked[:, :half]], axis=1)


def gradient_rows(resid_ref, xs_ref, mask_ref, rows):
    total = None
    for t in range(resid_ref.shape[0]):
        product = jnp.dot(resid_ref[t, 0, rows, :], xs_ref[2 * t], preferred_element_type=F32)
        product += jnp.dot(resid_ref[t, 1, rows, :], xs_ref[2 * t + 1], preferred_element_type=F32)
        part = twice(mask_ref[t, rows, :]) * product
        total = part if total is None else total + part
    return total


def half_start(index, rows):
    return pl.multiple_of(index * rows, rows)


def first_kernel(
    resid_hbm, flags_hbm, cluster_hbm, penalty_hbm, jones_hbm, duals_hbm,
    resid_ref, grad_ref, sent_ref, mask_ref, counts_ref, inverse_ref, rates_ref, duals_ref,
    flags_ref, cluster_ref, penalty_ref, jones_ref, xs_ref, sems,
):
    rows, cols = jones_ref.shape
    _, stations = flags_ref.shape
    share, own_rows = resid_ref.shape[0], duals_ref.shape[0]
    step = rows // PIECES
    cuts = [(sum(PARTS[:m]) * step, PARTS[m] * step) for m in range(len(PARTS))]
    own = pl.ds(half_start(lax.axis_index("tm"), own_rows), own_rows)
    small = [(flags_hbm, flags_ref), (cluster_hbm, cluster_ref), (penalty_hbm, penalty_ref)]
    pieces = small + [(jones_hbm, jones_ref), (duals_hbm.at[own, :], duals_ref)]
    for start, size in cuts:
        cut = pl.ds(start, size)
        pieces.append((resid_hbm.at[:, :, cut, :], resid_ref.at[:, :, cut, :]))
    copies = [pltpu.make_async_copy(src, dst, sems.at[k]) for k, (src, dst) in enumerate(pieces)]
    streams = copies[5:]
    for copy in copies[:4] + streams[:1] + copies[4:5] + streams[1:]:
        copy.start()

    for copy in copies[:3]:
        copy.wait()
    flags = flags_ref[...].astype(F32)
    pick = (
        lax.broadcasted_iota(jnp.int32, (rows, stations), 0) // 2
        == lax.broadcasted_iota(jnp.int32, (rows, stations), 1)
    ).astype(jnp.bfloat16)

    def rows_of(line):
        spread = jnp.broadcast_to(line, (LANES, stations)).astype(jnp.bfloat16)
        return lax.dot_general(pick, spread, (((1,), (1,)), ((), ())), preferred_element_type=F32)

    for t in range(share):
        line = flags_ref[pl.ds(lax.axis_index("tm") * share + t, 1), :].astype(F32)
        mask_ref[t] = rows_of(line)
    counts_ref[...] = rows_of(jnp.sum(flags, axis=0, keepdims=True))
    dirs = cluster_ref.shape[1]
    lane = lax.broadcasted_iota(jnp.int32, (dirs, cols), 1)
    spread = lax.rem(lane, cols // 2) // 2 == lax.broadcasted_iota(jnp.int32, (dirs, cols), 0)
    labels = jnp.broadcast_to(cluster_ref[...].astype(F32), (8, dirs)).astype(jnp.bfloat16)
    label = jnp.dot(labels, spread.astype(jnp.bfloat16), preferred_element_type=F32)
    rates = jnp.zeros((8, cols), F32)
    for k in range(penalty_ref.shape[1]):
        rates = jnp.where(label == k, penalty_ref[0:1, k : k + 1], rates)
    rates_ref[...] = rates
    inverse_ref[...] = 1.0 / (twice(counts_ref[...]) + rates[0:1])

    copies[3].wait()
    rounded = jones_ref[...].astype(jnp.bfloat16)
    for t in range(share):
        fill_operands(xs_ref, t, rounded, twice(mask_ref[t]))
    for m, (start, size) in enumerate(cuts):
        cut = pl.ds(start, size)
        streams[m].wait()
        total = gradient_rows(resid_ref, xs_ref, mask_ref, cut)
        if m == 0:
            copies[4].wait()
        half, offset = divmod(start, own_rows)
        mine = rates[0:1] * (lax.axis_index("tm") == half).astype(F32)
        total = total + mine * (jones_ref[cut, :] - duals_ref[offset : offset + size])
        grad_ref[cut, :] = total
        sent_ref[cut, :] = total.astype(WIRE)


def other_kernel(
    chunks, resid_ref, mine_ref, theirs_ref, mask_ref, inverse_ref, duals_ref,
    u_ref, other_ref, xs_ref,
):
    own_rows = u_ref.shape[0]
    jones = (mine_ref[...] + theirs_ref[...].astype(F32)) * inverse_ref[...]
    rounded = jones.astype(jnp.bfloat16)
    for t in range(resid_ref.shape[0]):
        fill_operands(xs_ref, t, rounded, twice(mask_ref[t]))
    own = pl.ds(half_start(lax.axis_index("tm"), own_rows), own_rows)
    u_ref[...] = (
        mine_ref[own, :] + theirs_ref[own, :].astype(F32)
    ) * inverse_ref[own, :] + duals_ref[...]
    step = own_rows // chunks
    for m in range(chunks):
        start = half_start(1 - lax.axis_index("tm"), own_rows) + m * step
        other_ref[m * step : (m + 1) * step] = gradient_rows(
            resid_ref, xs_ref, mask_ref, pl.ds(pl.multiple_of(start, step), step)
        )


def own_kernel(
    chunks, members, resid_ref, xs_ref, mask_ref, u_ref, counts_ref, own_ref, *message_refs
):
    own_rows = own_ref.shape[0]
    step = own_rows // chunks
    base = half_start(lax.axis_index("tm"), own_rows)
    for m in range(chunks):
        own_ref[m * step : (m + 1) * step] = gradient_rows(
            resid_ref, xs_ref, mask_ref, pl.ds(pl.multiple_of(base + m * step, step), step)
        )
    block = own_rows // members
    eye = eye_mask(block)
    for s, message in enumerate(message_refs):
        offset = half_start(lax.axis_index("chan") ^ s, block)
        message[0:block] = u_ref[pl.ds(offset, block), :].astype(WIRE)
        counts = counts_ref[pl.ds(pl.multiple_of(base + offset, block), block), :]
        line = jnp.sum(jnp.where(eye, counts, 0.0), axis=0, keepdims=True)
        message[2 * block : 2 * block + TILE, 0:LANES] = jnp.broadcast_to(line, (TILE, LANES)).astype(WIRE)


def pack_kernel(members, own_ref, theirs_ref, u_ref, inverse_ref, rates_ref, *refs):
    q_ref, message_refs = refs[members], refs[members + 1 :]
    own_rows = u_ref.shape[0]
    base = half_start(lax.axis_index("tm"), own_rows)
    block = own_rows // members
    rates = rates_ref[0:1]
    for s, message in enumerate(message_refs):
        offset = half_start(lax.axis_index("chan") ^ s, block)
        rows = pl.ds(offset, block)
        u = u_ref[rows, :]
        inverse = inverse_ref[pl.ds(pl.multiple_of(base + offset, block), block), :]
        q = (own_ref[rows, :] + theirs_ref[rows, :] - rates * u) * inverse
        q_ref[rows, :] = q
        message[block : 2 * block] = (u + q).astype(WIRE)


def owner_kernel(members, block, slots, rates_ref, *refs):
    received, returned = refs[:members], refs[members:]
    rates = rates_ref[0:1]
    eye = eye_mask(block)
    table = [2.0 * rates / (float(count) + rates) for count in range(slots + 1)]
    weights = [basis_at(lax.axis_index("chan") ^ s, members) for s in range(members)]
    coeffs = [None] * POLY
    sums = [None] * POLY
    plus = lambda a, b: b if a is None else a + b
    for s in range(members):
        u = received[s][0:block].astype(F32)
        w = received[s][block : 2 * block].astype(F32)
        for p in range(POLY):
            coeffs[p] = plus(coeffs[p], weights[s][p] * u)
            sums[p] = plus(sums[p], weights[s][p] * w)
    for s in range(members):
        line = received[s][2 * block : 2 * block + TILE, 0:LANES].astype(F32)[0:1]
        counts = jnp.sum(jnp.where(eye, line, 0.0), axis=1, keepdims=True)
        first = weights[s][0] * coeffs[0]
        for p in range(1, POLY):
            first = first + weights[s][p] * coeffs[p]
        returned[s][0:block] = first.astype(WIRE)
        weight = table[0]
        for count in range(1, slots + 1):
            weight = jnp.where(counts == count, table[count], weight)
        step = weight * first
        for p in range(POLY):
            sums[p] = sums[p] + weights[s][p] * step
    for s in range(members):
        second = weights[s][0] * sums[0]
        for p in range(1, POLY):
            second = second + weights[s][p] * sums[p]
        returned[s][block : 2 * block] = second.astype(WIRE)


def finish_kernel(members, group, q_ref, u_ref, inverse_ref, rates_ref, *refs):
    received = refs[: len(group)]
    jones_hbm, duals_hbm, jones_ref, duals_ref, sems = refs[-5:]
    rates = 2.0 * rates_ref[0:1]
    own_rows = u_ref.shape[0]
    block = own_rows // members
    base = half_start(lax.axis_index("tm"), own_rows)
    copies = []
    for k, s in enumerate(group):
        offset = half_start(lax.axis_index("chan") ^ s, block)
        rows = pl.ds(offset, block)
        inverse = inverse_ref[pl.ds(pl.multiple_of(base + offset, block), block), :]
        jones = q_ref[rows, :] + rates * inverse * received[k][0:block].astype(F32)
        jones_ref[k] = jones
        duals_ref[k] = u_ref[rows, :] + jones - received[k][block : 2 * block].astype(F32)
        for i, (src, dst) in enumerate(((jones_ref, jones_hbm), (duals_ref, duals_hbm))):
            copies.append(pltpu.make_async_copy(src.at[k], dst.at[rows, :], sems.at[i, k]))
            copies[-1].start()
    for copy in copies:
        copy.wait()


def shape_of(shape, dtype=F32):
    return jax.ShapeDtypeStruct(shape, dtype)


def in_vmem(shape, dtype=F32):
    return pltpu.VMEM(shape, dtype)


def call(kernel, outs, ins, limit, scratch=(), aliases={}, out_space=pltpu.VMEM):
    return pl.pallas_call(
        kernel, out_shape=tuple(outs), in_specs=[pl.BlockSpec(memory_space=space) for space in ins],
        out_specs=tuple(pl.BlockSpec(memory_space=out_space) for _ in outs), scratch_shapes=scratch,
        input_output_aliases=aliases,
        compiler_params=pltpu.CompilerParams(vmem_limit_bytes=limit * MIB),
    )


PIECES = 8
PARTS = (2, 2, 2, 1, 1)
CHUNKS = 2
EARLY = 3


def partner_order(members):
    return list(range(members - 1, 0, -1))


def on_device(residuals, flag_masks, cluster, penalty, jones_init, duals_init):
    members, halves = lax.axis_size("chan"), lax.axis_size("tm")
    share, rows = residuals.shape[1], residuals.shape[3]
    slots, cols = flag_masks.shape[1], jones_init.shape[2]
    own_rows = rows // halves
    block = own_rows // members
    vmem, hbm = pltpu.VMEM, pltpu.HBM
    bf16 = jnp.bfloat16

    resid, grad, sent, masks, counts, inverse, rates, duals0 = call(
        first_kernel,
        [
            in_vmem(residuals.shape[1:], bf16), in_vmem((rows, cols)), in_vmem((rows, cols), WIRE), in_vmem((share, rows, LANES)),
            in_vmem((rows, LANES)), in_vmem((rows, cols)), in_vmem((8, cols)), in_vmem((own_rows, cols)),
        ],
        [hbm] * 6, 40,
        [
            vmem((slots, rows // 2), jnp.int32), vmem((1, cluster.shape[0]), jnp.int32),
            vmem((1, penalty.shape[0]), F32), vmem((rows, cols), F32), vmem((2 * share, rows, cols), bf16),
            pltpu.SemaphoreType.DMA((5 + len(PARTS),)),
        ],
    )(*(
        pltpu.with_memory_space_constraint(x, hbm)
        for x in (residuals[0], flag_masks[0], cluster[None, :], penalty[None, :], jones_init[0], duals_init[0])
    ))

    swap = [(0, 1), (1, 0)]
    grad_other = lax.ppermute(sent, "tm", swap)
    u, other, xs = call(
        functools.partial(other_kernel, CHUNKS),
        [in_vmem((own_rows, cols)), in_vmem((own_rows, cols)), in_vmem((2 * share, rows, cols), bf16)],
        [vmem] * 6, 24,
    )(resid, grad, grad_other, masks, inverse, duals0)
    theirs = lax.ppermute(other, "tm", swap)
    message = in_vmem((2 * block + TILE, cols), WIRE)
    own, *messages = call(
        functools.partial(own_kernel, CHUNKS, members),
        [in_vmem((own_rows, cols))] + [message] * members, [vmem] * 5, 24,
    )(resid, xs, masks, u, counts)
    q, *messages = call(
        functools.partial(pack_kernel, members), [in_vmem((own_rows, cols))] + [message] * members,
        [vmem] * (5 + members), 16, aliases={5 + s: 1 + s for s in range(members)},
    )(own, theirs, u, inverse, rates, *messages)

    def exchange(parts):
        got = [None] * members
        got[0] = parts[0]
        for s in partner_order(members):
            got[s] = lax.ppermute(parts[s], "chan", [(f, f ^ s) for f in range(members)])
        return got

    messages = exchange(messages)
    returned = call(
        functools.partial(owner_kernel, members, block, slots),
        [shape_of((2 * block, cols), WIRE)] * members, [vmem] * (1 + members), 16,
    )(rates, *messages)
    returned = exchange(returned)
    order = [0] + partner_order(members)
    early = len(order) * EARLY // 8
    outputs = []
    for group in (order[:early], order[early:]):
        spaces = [vmem] * (4 + len(group)) + [hbm] * len(outputs)
        outputs = call(
            functools.partial(finish_kernel, members, group),
            [shape_of((own_rows, cols))] * 2, spaces, 16,
            [
                vmem((len(group), block, cols), F32), vmem((len(group), block, cols), F32),
                pltpu.SemaphoreType.DMA((2, len(group))),
            ],
            {4 + len(group) + i: i for i in range(len(outputs))}, hbm,
        )(q, u, inverse, rates, *(returned[s] for s in group), *outputs)
    return outputs[0][None], outputs[1][None]


def solution(mesh):
    in_specs = (
        P(("obs", "chan"), "tm", None, None, None),
        P(("obs", "chan"), None, None),
        P("obs"),
        P("obs"),
        P(("obs", "chan"), None, None),
        P(("obs", "chan"), None, None),
    )
    out_specs = (P(("obs", "chan"), "tm", None), P(("obs", "chan"), "tm", None))
    return jax.shard_map(
        on_device, mesh=mesh, in_specs=in_specs, out_specs=out_specs, check_vma=False
    )
```

```python
import functools

import jax
import jax.numpy as jnp
import numpy as np
from jax import lax
from jax.experimental import pallas as pl
from jax.experimental.pallas import tpu as pltpu
from jax.sharding import PartitionSpec as P


POLY = 3
WIRE = jnp.bfloat16
F32 = jnp.float32
LANES = 128
TILE = 8
MIB = 1 << 20


def poly_basis(total_count):
    position = (2.0 * np.arange(total_count) + 1.0) / total_count - 1.0
    powers = np.stack([position**degree for degree in range(POLY)], axis=1)
    columns = []
    for degree in range(POLY):
        column = np.eye(POLY)[degree]
        for previous in columns:
            column = column - np.sum((powers @ column) * (powers @ previous)) * previous
        columns.append(column / np.sqrt(np.sum((powers @ column) ** 2)))
    return columns


def basis_at(channel, total_count):
    position = (2.0 * channel.astype(F32) + 1.0) * (1.0 / total_count) - 1.0
    values = []
    for column in poly_basis(total_count):
        value = jnp.float32(column[POLY - 1])
        for coefficient in column[POLY - 2 :: -1]:
            value = value * position + np.float32(coefficient)
        values.append(value)
    return values


def eye_mask(rows):
    shape = (rows, max(rows, LANES))
    return lax.broadcasted_iota(jnp.int32, shape, 0) == lax.broadcasted_iota(jnp.int32, shape, 1)


def twice(half):
    return jnp.concatenate([half, half], axis=1)


def fill_operands(xs_ref, slot, rounded, mask):
    half = rounded.shape[1] // 2
    masked = mask.astype(jnp.bfloat16) * rounded
    xs_ref[2 * slot] = masked
    xs_ref[2 * slot + 1] = jnp.concatenate([-masked[:, half:], masked[:, :half]], axis=1)


def gradient_rows(resid_ref, xs_ref, mask_ref, rows):
    total = None
    for t in range(resid_ref.shape[0]):
        product = jnp.dot(resid_ref[t, 0, rows, :], xs_ref[2 * t], preferred_element_type=F32)
        product += jnp.dot(resid_ref[t, 1, rows, :], xs_ref[2 * t + 1], preferred_element_type=F32)
        part = twice(mask_ref[t, rows, :]) * product
        total = part if total is None else total + part
    return total


def store_wide(message, first, block, value):
    for k in range(value.shape[1] // LANES):
        message[first + k * block : first + (k + 1) * block] = value[:, k * LANES : (k + 1) * LANES].astype(WIRE)


def load_wide(message, first, block, cols):
    return jnp.concatenate(
        [message[first + k * block : first + (k + 1) * block].astype(F32) for k in range(cols // LANES)], axis=1
    )


def half_start(index, rows):
    return pl.multiple_of(index * rows, rows)


def first_kernel(
    resid_hbm, flags_hbm, cluster_hbm, penalty_hbm, jones_hbm, duals_hbm,
    resid_ref, grad_ref, sent_ref, mask_ref, counts_ref, inverse_ref, rates_ref, duals_ref,
    flags_ref, cluster_ref, penalty_ref, jones_ref, xs_ref, sems,
):
    rows, cols = jones_ref.shape
    _, stations = flags_ref.shape
    share, own_rows = resid_ref.shape[0], duals_ref.shape[0]
    step = rows // PIECES
    cuts = [(sum(PARTS[:m]) * step, PARTS[m] * step) for m in range(len(PARTS))]
    own = pl.ds(half_start(lax.axis_index("tm"), own_rows), own_rows)
    small = [(flags_hbm, flags_ref), (cluster_hbm, cluster_ref), (penalty_hbm, penalty_ref)]
    pieces = small + [(jones_hbm, jones_ref), (duals_hbm.at[own, :], duals_ref)]
    for start, size in cuts:
        cut = pl.ds(start, size)
        pieces.append((resid_hbm.at[:, :, cut, :], resid_ref.at[:, :, cut, :]))
    copies = [pltpu.make_async_copy(src, dst, sems.at[k]) for k, (src, dst) in enumerate(pieces)]
    streams = copies[5:]
    for copy in copies[:4] + streams[:1] + copies[4:5] + streams[1:]:
        copy.start()

    for copy in copies[:3]:
        copy.wait()
    flags = flags_ref[...].astype(F32)
    pick = (
        lax.broadcasted_iota(jnp.int32, (rows, stations), 0) // 2
        == lax.broadcasted_iota(jnp.int32, (rows, stations), 1)
    ).astype(jnp.bfloat16)

    def rows_of(line):
        spread = jnp.broadcast_to(line, (LANES, stations)).astype(jnp.bfloat16)
        return lax.dot_general(pick, spread, (((1,), (1,)), ((), ())), preferred_element_type=F32)

    for t in range(share):
        line = flags_ref[pl.ds(lax.axis_index("tm") * share + t, 1), :].astype(F32)
        mask_ref[t] = rows_of(line)
    counts_ref[...] = rows_of(jnp.sum(flags, axis=0, keepdims=True))
    dirs = cluster_ref.shape[1]
    lane = lax.broadcasted_iota(jnp.int32, (dirs, cols), 1)
    spread = lax.rem(lane, cols // 2) // 2 == lax.broadcasted_iota(jnp.int32, (dirs, cols), 0)
    labels = jnp.broadcast_to(cluster_ref[...].astype(F32), (8, dirs)).astype(jnp.bfloat16)
    label = jnp.dot(labels, spread.astype(jnp.bfloat16), preferred_element_type=F32)
    rates = jnp.zeros((8, cols), F32)
    for k in range(penalty_ref.shape[1]):
        rates = jnp.where(label == k, penalty_ref[0:1, k : k + 1], rates)
    rates_ref[...] = rates
    inverse_ref[...] = 1.0 / (twice(counts_ref[...]) + rates[0:1])

    copies[3].wait()
    rounded = jones_ref[...].astype(jnp.bfloat16)
    for t in range(share):
        fill_operands(xs_ref, t, rounded, twice(mask_ref[t]))
    for m, (start, size) in enumerate(cuts):
        cut = pl.ds(start, size)
        streams[m].wait()
        total = gradient_rows(resid_ref, xs_ref, mask_ref, cut)
        if m == 0:
            copies[4].wait()
        half, offset = divmod(start, own_rows)
        mine = rates[0:1] * (lax.axis_index("tm") == half).astype(F32)
        total = total + mine * (jones_ref[cut, :] - duals_ref[offset : offset + size])
        grad_ref[cut, :] = total
        sent_ref[cut, :] = total.astype(WIRE)


def other_kernel(
    chunks, resid_ref, mine_ref, theirs_ref, mask_ref, inverse_ref, duals_ref,
    u_ref, other_ref, xs_ref,
):
    own_rows = u_ref.shape[0]
    jones = (mine_ref[...] + theirs_ref[...].astype(F32)) * inverse_ref[...]
    rounded = jones.astype(jnp.bfloat16)
    for t in range(resid_ref.shape[0]):
        fill_operands(xs_ref, t, rounded, twice(mask_ref[t]))
    own = pl.ds(half_start(lax.axis_index("tm"), own_rows), own_rows)
    u_ref[...] = (
        mine_ref[own, :] + theirs_ref[own, :].astype(F32)
    ) * inverse_ref[own, :] + duals_ref[...]
    step = own_rows // chunks
    for m in range(chunks):
        start = half_start(1 - lax.axis_index("tm"), own_rows) + m * step
        other_ref[m * step : (m + 1) * step] = gradient_rows(
            resid_ref, xs_ref, mask_ref, pl.ds(pl.multiple_of(start, step), step)
        )


def own_kernel(
    chunks, members, resid_ref, xs_ref, mask_ref, u_ref, counts_ref, own_ref, *message_refs
):
    own_rows = own_ref.shape[0]
    step = own_rows // chunks
    base = half_start(lax.axis_index("tm"), own_rows)
    for m in range(chunks):
        own_ref[m * step : (m + 1) * step] = gradient_rows(
            resid_ref, xs_ref, mask_ref, pl.ds(pl.multiple_of(base + m * step, step), step)
        )
    block = own_rows // members
    eye = eye_mask(block)
    for s, message in enumerate(message_refs):
        offset = half_start(lax.axis_index("chan") ^ s, block)
        store_wide(message, 0, block, u_ref[pl.ds(offset, block), :])
        counts = counts_ref[pl.ds(pl.multiple_of(base + offset, block), block), :]
        line = jnp.sum(jnp.where(eye, counts, 0.0), axis=0, keepdims=True)
        first = 2 * block * (u_ref.shape[1] // LANES)
        message[first : first + TILE] = jnp.broadcast_to(line, (TILE, LANES)).astype(WIRE)


def pack_kernel(members, own_ref, theirs_ref, u_ref, inverse_ref, rates_ref, *refs):
    q_ref, message_refs = refs[members], refs[members + 1 :]
    own_rows = u_ref.shape[0]
    base = half_start(lax.axis_index("tm"), own_rows)
    block = own_rows // members
    rates = rates_ref[0:1]
    for s, message in enumerate(message_refs):
        offset = half_start(lax.axis_index("chan") ^ s, block)
        rows = pl.ds(offset, block)
        u = u_ref[rows, :]
        inverse = inverse_ref[pl.ds(pl.multiple_of(base + offset, block), block), :]
        q = (own_ref[rows, :] + theirs_ref[rows, :] - rates * u) * inverse
        q_ref[rows, :] = q
        store_wide(message, block * (u.shape[1] // LANES), block, u + q)


def owner_kernel(members, block, slots, rates_ref, *refs):
    received, returned = refs[:members], refs[members:]
    rates, cols = rates_ref[0:1], rates_ref.shape[1]
    eye = eye_mask(block)
    table = [2.0 * rates / (float(count) + rates) for count in range(slots + 1)]
    weights = [basis_at(lax.axis_index("chan") ^ s, members) for s in range(members)]
    coeffs = [None] * POLY
    sums = [None] * POLY
    plus = lambda a, b: b if a is None else a + b
    for s in range(members):
        u = load_wide(received[s], 0, block, cols)
        w = load_wide(received[s], block * (cols // LANES), block, cols)
        for p in range(POLY):
            coeffs[p] = plus(coeffs[p], weights[s][p] * u)
            sums[p] = plus(sums[p], weights[s][p] * w)
    for s in range(members):
        first = 2 * block * (cols // LANES)
        line = received[s][first : first + TILE].astype(F32)[0:1]
        counts = jnp.sum(jnp.where(eye, line, 0.0), axis=1, keepdims=True)
        first = weights[s][0] * coeffs[0]
        for p in range(1, POLY):
            first = first + weights[s][p] * coeffs[p]
        returned[s][0:block] = first.astype(WIRE)
        weight = table[0]
        for count in range(1, slots + 1):
            weight = jnp.where(counts == count, table[count], weight)
        step = weight * first
        for p in range(POLY):
            sums[p] = sums[p] + weights[s][p] * step
    for s in range(members):
        second = weights[s][0] * sums[0]
        for p in range(1, POLY):
            second = second + weights[s][p] * sums[p]
        returned[s][block : 2 * block] = second.astype(WIRE)


def finish_kernel(members, group, q_ref, u_ref, inverse_ref, rates_ref, *refs):
    received = refs[: len(group)]
    jones_hbm, duals_hbm, jones_ref, duals_ref, sems = refs[-5:]
    rates = 2.0 * rates_ref[0:1]
    own_rows = u_ref.shape[0]
    block = own_rows // members
    base = half_start(lax.axis_index("tm"), own_rows)
    copies = []
    for k, s in enumerate(group):
        offset = half_start(lax.axis_index("chan") ^ s, block)
        rows = pl.ds(offset, block)
        inverse = inverse_ref[pl.ds(pl.multiple_of(base + offset, block), block), :]
        jones = q_ref[rows, :] + rates * inverse * received[k][0:block].astype(F32)
        jones_ref[k] = jones
        duals_ref[k] = u_ref[rows, :] + jones - received[k][block : 2 * block].astype(F32)
        for i, (src, dst) in enumerate(((jones_ref, jones_hbm), (duals_ref, duals_hbm))):
            copies.append(pltpu.make_async_copy(src.at[k], dst.at[rows, :], sems.at[i, k]))
            copies[-1].start()
    for copy in copies:
        copy.wait()


def shape_of(shape, dtype=F32):
    return jax.ShapeDtypeStruct(shape, dtype)


def in_vmem(shape, dtype=F32):
    return pltpu.VMEM(shape, dtype)


def call(kernel, outs, ins, limit, scratch=(), aliases={}, out_space=pltpu.VMEM):
    return pl.pallas_call(
        kernel, out_shape=tuple(outs), in_specs=[pl.BlockSpec(memory_space=space) for space in ins],
        out_specs=tuple(pl.BlockSpec(memory_space=out_space) for _ in outs), scratch_shapes=scratch,
        input_output_aliases=aliases,
        compiler_params=pltpu.CompilerParams(vmem_limit_bytes=limit * MIB),
    )


PIECES = 8
PARTS = (2, 2, 2, 2)
CHUNKS = 1
EARLY = 3


def partner_order(members):
    far = list(range(members - 1, members // 2 - 1, -1))
    near = list(range(members // 2 - 1, 0, -1))
    return far[:1] + [partner for pair in zip(far[1:], near) for partner in pair]


def on_device(residuals, flag_masks, cluster, penalty, jones_init, duals_init):
    members, halves = lax.axis_size("chan"), lax.axis_size("tm")
    share, rows = residuals.shape[1], residuals.shape[3]
    slots, cols = flag_masks.shape[1], jones_init.shape[2]
    own_rows = rows // halves
    block = own_rows // members
    vmem, hbm = pltpu.VMEM, pltpu.HBM
    bf16 = jnp.bfloat16

    resid, grad, sent, masks, counts, inverse, rates, duals0 = call(
        first_kernel,
        [
            in_vmem(residuals.shape[1:], bf16), in_vmem((rows, cols)), in_vmem((rows, cols), WIRE), in_vmem((share, rows, LANES)),
            in_vmem((rows, LANES)), in_vmem((rows, cols)), in_vmem((8, cols)), in_vmem((own_rows, cols)),
        ],
        [hbm] * 6, 40,
        [
            vmem((slots, rows // 2), jnp.int32), vmem((1, cluster.shape[0]), jnp.int32),
            vmem((1, penalty.shape[0]), F32), vmem((rows, cols), F32), vmem((2 * share, rows, cols), bf16),
            pltpu.SemaphoreType.DMA((5 + len(PARTS),)),
        ],
    )(*(
        pltpu.with_memory_space_constraint(x, hbm)
        for x in (residuals[0], flag_masks[0], cluster[None, :], penalty[None, :], jones_init[0], duals_init[0])
    ))

    swap = [(0, 1), (1, 0)]
    grad_other = lax.ppermute(sent, "tm", swap)
    u, other, xs = call(
        functools.partial(other_kernel, CHUNKS),
        [in_vmem((own_rows, cols)), in_vmem((own_rows, cols)), in_vmem((2 * share, rows, cols), bf16)],
        [vmem] * 6, 24,
    )(resid, grad, grad_other, masks, inverse, duals0)
    theirs = lax.ppermute(other, "tm", swap)
    message = in_vmem((2 * block * (cols // LANES) + TILE, LANES), WIRE)
    own, *messages = call(
        functools.partial(own_kernel, CHUNKS, members),
        [in_vmem((own_rows, cols))] + [message] * members, [vmem] * 5, 24,
    )(resid, xs, masks, u, counts)
    q, *messages = call(
        functools.partial(pack_kernel, members), [in_vmem((own_rows, cols))] + [message] * members,
        [vmem] * (5 + members), 16, aliases={5 + s: 1 + s for s in range(members)},
    )(own, theirs, u, inverse, rates, *messages)

    def exchange(parts):
        got = [None] * members
        got[0] = parts[0]
        for s in partner_order(members):
            got[s] = lax.ppermute(parts[s], "chan", [(f, f ^ s) for f in range(members)])
        return got

    messages = exchange(messages)
    returned = call(
        functools.partial(owner_kernel, members, block, slots),
        [shape_of((2 * block, cols), WIRE)] * members, [vmem] * (1 + members), 16,
    )(rates, *messages)
    returned = exchange(returned)
    order = [0] + partner_order(members)
    early = len(order) * EARLY // 8
    outputs = []
    for group in (order[:early], order[early:]):
        spaces = [vmem] * (4 + len(group)) + [hbm] * len(outputs)
        outputs = call(
            functools.partial(finish_kernel, members, group),
            [shape_of((own_rows, cols))] * 2, spaces, 16,
            [
                vmem((len(group), block, cols), F32), vmem((len(group), block, cols), F32),
                pltpu.SemaphoreType.DMA((2, len(group))),
            ],
            {4 + len(group) + i: i for i in range(len(outputs))}, hbm,
        )(q, u, inverse, rates, *(returned[s] for s in group), *outputs)
    return outputs[0][None], outputs[1][None]


def solution(mesh):
    in_specs = (
        P(("obs", "chan"), "tm", None, None, None),
        P(("obs", "chan"), None, None),
        P("obs"),
        P("obs"),
        P(("obs", "chan"), None, None),
        P(("obs", "chan"), None, None),
    )
    out_specs = (P(("obs", "chan"), "tm", None), P(("obs", "chan"), "tm", None))
    return jax.shard_map(
        on_device, mesh=mesh, in_specs=in_specs, out_specs=out_specs, check_vma=False
    )
```

```python
import functools

import jax
import jax.numpy as jnp
import numpy as np
from jax import lax
from jax.experimental import pallas as pl
from jax.experimental.pallas import tpu as pltpu
from jax.sharding import PartitionSpec as P


POLY = 3
WIRE = jnp.bfloat16
F32 = jnp.float32
LANES = 128
TILE = 8
MIB = 1 << 20


def poly_basis(total_count):
    position = (2.0 * np.arange(total_count) + 1.0) / total_count - 1.0
    powers = np.stack([position**degree for degree in range(POLY)], axis=1)
    columns = []
    for degree in range(POLY):
        column = np.eye(POLY)[degree]
        for previous in columns:
            column = column - np.sum((powers @ column) * (powers @ previous)) * previous
        columns.append(column / np.sqrt(np.sum((powers @ column) ** 2)))
    return columns


def basis_at(channel, total_count):
    position = (2.0 * channel.astype(F32) + 1.0) * (1.0 / total_count) - 1.0
    values = []
    for column in poly_basis(total_count):
        value = jnp.float32(column[POLY - 1])
        for coefficient in column[POLY - 2 :: -1]:
            value = value * position + np.float32(coefficient)
        values.append(value)
    return values


def eye_mask(rows):
    shape = (rows, max(rows, LANES))
    return lax.broadcasted_iota(jnp.int32, shape, 0) == lax.broadcasted_iota(jnp.int32, shape, 1)


def twice(half):
    return jnp.concatenate([half, half], axis=1)


def fill_operands(xs_ref, slot, rounded, mask):
    half = rounded.shape[1] // 2
    masked = mask.astype(jnp.bfloat16) * rounded
    xs_ref[2 * slot] = masked
    xs_ref[2 * slot + 1] = jnp.concatenate([-masked[:, half:], masked[:, :half]], axis=1)


def gradient_rows(resid_ref, xs_ref, mask_ref, rows):
    total = None
    for t in range(resid_ref.shape[0]):
        product = jnp.dot(resid_ref[t, 0, rows, :], xs_ref[2 * t], preferred_element_type=F32)
        product += jnp.dot(resid_ref[t, 1, rows, :], xs_ref[2 * t + 1], preferred_element_type=F32)
        part = twice(mask_ref[t, rows, :]) * product
        total = part if total is None else total + part
    return total


def store_wide(message, first, block, value):
    for k in range(value.shape[1] // LANES):
        message[first + k * block : first + (k + 1) * block] = value[:, k * LANES : (k + 1) * LANES].astype(WIRE)


def half_start(index, rows):
    return pl.multiple_of(index * rows, rows)


def first_kernel(
    resid_hbm, flags_hbm, cluster_hbm, penalty_hbm, jones_hbm, duals_hbm,
    resid_ref, grad_ref, sent_ref, mask_ref, counts_ref, inverse_ref, rates_ref, duals_ref,
    flags_ref, cluster_ref, penalty_ref, jones_ref, xs_ref, sems,
):
    rows, cols = jones_ref.shape
    _, stations = flags_ref.shape
    share, own_rows = resid_ref.shape[0], duals_ref.shape[0]
    step = rows // PIECES
    cuts = [(sum(PARTS[:m]) * step, PARTS[m] * step) for m in range(len(PARTS))]
    own = pl.ds(half_start(lax.axis_index("tm"), own_rows), own_rows)
    small = [(flags_hbm, flags_ref), (cluster_hbm, cluster_ref), (penalty_hbm, penalty_ref)]
    pieces = small + [(jones_hbm, jones_ref), (duals_hbm.at[own, :], duals_ref)]
    for start, size in cuts:
        cut = pl.ds(start, size)
        pieces.append((resid_hbm.at[:, :, cut, :], resid_ref.at[:, :, cut, :]))
    copies = [pltpu.make_async_copy(src, dst, sems.at[k]) for k, (src, dst) in enumerate(pieces)]
    streams = copies[5:]
    for copy in copies[:4] + streams[:1] + copies[4:5] + streams[1:]:
        copy.start()

    for copy in copies[:3]:
        copy.wait()
    flags = flags_ref[...].astype(F32)
    pick = (
        lax.broadcasted_iota(jnp.int32, (rows, stations), 0) // 2
        == lax.broadcasted_iota(jnp.int32, (rows, stations), 1)
    ).astype(jnp.bfloat16)

    def rows_of(line):
        spread = jnp.broadcast_to(line, (LANES, stations)).astype(jnp.bfloat16)
        return lax.dot_general(pick, spread, (((1,), (1,)), ((), ())), preferred_element_type=F32)

    for t in range(share):
        line = flags_ref[pl.ds(lax.axis_index("tm") * share + t, 1), :].astype(F32)
        mask_ref[t] = rows_of(line)
    counts_ref[...] = rows_of(jnp.sum(flags, axis=0, keepdims=True))
    dirs = cluster_ref.shape[1]
    lane = lax.broadcasted_iota(jnp.int32, (dirs, cols), 1)
    spread = lax.rem(lane, cols // 2) // 2 == lax.broadcasted_iota(jnp.int32, (dirs, cols), 0)
    labels = jnp.broadcast_to(cluster_ref[...].astype(F32), (8, dirs)).astype(jnp.bfloat16)
    label = jnp.dot(labels, spread.astype(jnp.bfloat16), preferred_element_type=F32)
    rates = jnp.zeros((8, cols), F32)
    for k in range(penalty_ref.shape[1]):
        rates = jnp.where(label == k, penalty_ref[0:1, k : k + 1], rates)
    rates_ref[...] = rates
    inverse_ref[...] = 1.0 / (twice(counts_ref[...]) + rates[0:1])

    copies[3].wait()
    rounded = jones_ref[...].astype(jnp.bfloat16)
    for t in range(share):
        fill_operands(xs_ref, t, rounded, twice(mask_ref[t]))
    for m, (start, size) in enumerate(cuts):
        cut = pl.ds(start, size)
        streams[m].wait()
        total = gradient_rows(resid_ref, xs_ref, mask_ref, cut)
        if m == 0:
            copies[4].wait()
        half, offset = divmod(start, own_rows)
        mine = rates[0:1] * (lax.axis_index("tm") == half).astype(F32)
        total = total + mine * (jones_ref[cut, :] - duals_ref[offset : offset + size])
        grad_ref[cut, :] = total
        sent_ref[cut, :] = total.astype(WIRE)


def other_kernel(
    chunks, resid_ref, mine_ref, theirs_ref, mask_ref, inverse_ref, duals_ref,
    u_ref, other_ref, xs_ref,
):
    own_rows = u_ref.shape[0]
    jones = (mine_ref[...] + theirs_ref[...].astype(F32)) * inverse_ref[...]
    rounded = jones.astype(jnp.bfloat16)
    for t in range(resid_ref.shape[0]):
        fill_operands(xs_ref, t, rounded, twice(mask_ref[t]))
    own = pl.ds(half_start(lax.axis_index("tm"), own_rows), own_rows)
    u_ref[...] = (
        mine_ref[own, :] + theirs_ref[own, :].astype(F32)
    ) * inverse_ref[own, :] + duals_ref[...]
    step = own_rows // chunks
    for m in range(chunks):
        start = half_start(1 - lax.axis_index("tm"), own_rows) + m * step
        other_ref[m * step : (m + 1) * step] = gradient_rows(
            resid_ref, xs_ref, mask_ref, pl.ds(pl.multiple_of(start, step), step)
        )


def own_kernel(
    chunks, members, resid_ref, xs_ref, mask_ref, u_ref, counts_ref, own_ref, *message_refs
):
    own_rows = own_ref.shape[0]
    step = own_rows // chunks
    base = half_start(lax.axis_index("tm"), own_rows)
    for m in range(chunks):
        own_ref[m * step : (m + 1) * step] = gradient_rows(
            resid_ref, xs_ref, mask_ref, pl.ds(pl.multiple_of(base + m * step, step), step)
        )
    block = own_rows // members
    eye = eye_mask(block)
    for s, message in enumerate(message_refs):
        offset = half_start(lax.axis_index("chan") ^ s, block)
        store_wide(message, 0, block, u_ref[pl.ds(offset, block), :])
        counts = counts_ref[pl.ds(pl.multiple_of(base + offset, block), block), :]
        line = jnp.sum(jnp.where(eye, counts, 0.0), axis=0, keepdims=True)
        first = 2 * block * (u_ref.shape[1] // LANES)
        message[first : first + TILE] = jnp.broadcast_to(line, (TILE, LANES)).astype(WIRE)


def pack_kernel(members, own_ref, theirs_ref, u_ref, inverse_ref, rates_ref, *refs):
    q_ref, message_refs = refs[members], refs[members + 1 :]
    own_rows = u_ref.shape[0]
    base = half_start(lax.axis_index("tm"), own_rows)
    block = own_rows // members
    rates = rates_ref[0:1]
    for s, message in enumerate(message_refs):
        offset = half_start(lax.axis_index("chan") ^ s, block)
        rows = pl.ds(offset, block)
        u = u_ref[rows, :]
        inverse = inverse_ref[pl.ds(pl.multiple_of(base + offset, block), block), :]
        q = (own_ref[rows, :] + theirs_ref[rows, :] - rates * u) * inverse
        q_ref[rows, :] = q
        store_wide(message, block * (u.shape[1] // LANES), block, u + q)


def self_share(weights):
    return sum(weight * weight for weight in weights[1:]) + weights[0] * weights[0]


def owner_kernel(members, block, slots, rates_ref, *refs):
    received, returned = refs[:members], refs[members:]
    rates, cols = rates_ref[0:1], rates_ref.shape[1]
    eye = eye_mask(block)
    table = [2.0 * rates / (float(count) + rates) for count in range(slots + 1)]
    weights = [basis_at(lax.axis_index("chan") ^ s, members) for s in range(members)]
    shares = [self_share(weight) for weight in weights]
    pieces = cols // LANES
    ends = 2 * block * pieces
    usable = []
    for s in range(members):
        line = received[s][ends : ends + TILE].astype(F32)[0:1]
        usable.append(jnp.sum(jnp.where(eye, line, 0.0), axis=1, keepdims=True))

    def combine(terms):
        total = terms[0]
        for term in terms[1:]:
            total = total + term
        return total

    for row in range(0, block, 2 * TILE):
        for k in range(pieces):
            lanes = slice(k * LANES, (k + 1) * LANES)
            here = slice(k * block + row, k * block + row + 2 * TILE)
            there = slice((pieces + k) * block + row, (pieces + k) * block + row + 2 * TILE)
            u = [received[s][here].astype(F32) for s in range(members)]
            coeffs = [combine([weights[s][p] * u[s] for s in range(members)]) for p in range(POLY)]
            w = [received[s][there].astype(F32) for s in range(members)]
            known = []
            for s in range(members):
                first = combine([weights[s][p] * coeffs[p] for p in range(POLY)])
                returned[s][row : row + 2 * TILE, lanes] = (first - shares[s] * u[s]).astype(WIRE)
                counts = usable[s][row : row + 2 * TILE]
                weight = table[0][:, lanes]
                for count in range(1, slots + 1):
                    weight = jnp.where(counts == count, table[count][:, lanes], weight)
                step = weight * first
                known.append(shares[s] * w[s] + step)
                w[s] = w[s] + step
            sums = [combine([weights[s][p] * w[s] for s in range(members)]) for p in range(POLY)]
            for s in range(members):
                second = combine([weights[s][p] * sums[p] for p in range(POLY)])
                returned[s][block + row : block + row + 2 * TILE, lanes] = (second - known[s]).astype(WIRE)


def finish_kernel(members, group, q_ref, u_ref, inverse_ref, rates_ref, *refs):
    received = refs[: len(group)]
    jones_hbm, duals_hbm, jones_ref, duals_ref, sems = refs[-5:]
    rates = 2.0 * rates_ref[0:1]
    share = self_share(basis_at(lax.axis_index("chan"), members))
    own_rows = u_ref.shape[0]
    block = own_rows // members
    base = half_start(lax.axis_index("tm"), own_rows)
    copies = []
    for k, s in enumerate(group):
        offset = half_start(lax.axis_index("chan") ^ s, block)
        rows = pl.ds(offset, block)
        inverse = inverse_ref[pl.ds(pl.multiple_of(base + offset, block), block), :]
        u, q = u_ref[rows, :], q_ref[rows, :]
        first = received[k][0:block].astype(F32) + share * u
        jones_ref[k] = q + rates * inverse * first
        duals_ref[k] = (1.0 - share) * (u + q) - received[k][block : 2 * block].astype(F32)
        for i, (src, dst) in enumerate(((jones_ref, jones_hbm), (duals_ref, duals_hbm))):
            copies.append(pltpu.make_async_copy(src.at[k], dst.at[rows, :], sems.at[i, k]))
            copies[-1].start()
    for copy in copies:
        copy.wait()


def shape_of(shape, dtype=F32):
    return jax.ShapeDtypeStruct(shape, dtype)


def in_vmem(shape, dtype=F32):
    return pltpu.VMEM(shape, dtype)


def call(kernel, outs, ins, limit, scratch=(), aliases={}, out_space=pltpu.VMEM):
    return pl.pallas_call(
        kernel, out_shape=tuple(outs), in_specs=[pl.BlockSpec(memory_space=space) for space in ins],
        out_specs=tuple(pl.BlockSpec(memory_space=out_space) for _ in outs), scratch_shapes=scratch,
        input_output_aliases=aliases,
        compiler_params=pltpu.CompilerParams(vmem_limit_bytes=limit * MIB),
    )


PIECES = 8
PARTS = (2, 2, 2, 2)
CHUNKS = 1
EARLY = 3


def partner_order(members):
    far = list(range(members - 1, members // 2 - 1, -1))
    near = list(range(members // 2 - 1, 0, -1))
    return far[:1] + [partner for pair in zip(far[1:], near) for partner in pair]


def on_device(residuals, flag_masks, cluster, penalty, jones_init, duals_init):
    members, halves = lax.axis_size("chan"), lax.axis_size("tm")
    share, rows = residuals.shape[1], residuals.shape[3]
    slots, cols = flag_masks.shape[1], jones_init.shape[2]
    own_rows = rows // halves
    block = own_rows // members
    vmem, hbm = pltpu.VMEM, pltpu.HBM
    bf16 = jnp.bfloat16

    resid, grad, sent, masks, counts, inverse, rates, duals0 = call(
        first_kernel,
        [
            in_vmem(residuals.shape[1:], bf16), in_vmem((rows, cols)), in_vmem((rows, cols), WIRE), in_vmem((share, rows, LANES)),
            in_vmem((rows, LANES)), in_vmem((rows, cols)), in_vmem((8, cols)), in_vmem((own_rows, cols)),
        ],
        [hbm] * 6, 40,
        [
            vmem((slots, rows // 2), jnp.int32), vmem((1, cluster.shape[0]), jnp.int32),
            vmem((1, penalty.shape[0]), F32), vmem((rows, cols), F32), vmem((2 * share, rows, cols), bf16),
            pltpu.SemaphoreType.DMA((5 + len(PARTS),)),
        ],
    )(*(
        pltpu.with_memory_space_constraint(x, hbm)
        for x in (residuals[0], flag_masks[0], cluster[None, :], penalty[None, :], jones_init[0], duals_init[0])
    ))

    swap = [(0, 1), (1, 0)]
    grad_other = lax.ppermute(sent, "tm", swap)
    u, other, xs = call(
        functools.partial(other_kernel, CHUNKS),
        [in_vmem((own_rows, cols)), in_vmem((own_rows, cols)), in_vmem((2 * share, rows, cols), bf16)],
        [vmem] * 6, 24,
    )(resid, grad, grad_other, masks, inverse, duals0)
    theirs = lax.ppermute(other, "tm", swap)
    message = in_vmem((2 * block * (cols // LANES) + TILE, LANES), WIRE)
    own, *messages = call(
        functools.partial(own_kernel, CHUNKS, members),
        [in_vmem((own_rows, cols))] + [message] * members, [vmem] * 5, 24,
    )(resid, xs, masks, u, counts)
    q, *messages = call(
        functools.partial(pack_kernel, members), [in_vmem((own_rows, cols))] + [message] * members,
        [vmem] * (5 + members), 16, aliases={5 + s: 1 + s for s in range(members)},
    )(own, theirs, u, inverse, rates, *messages)

    def exchange(parts):
        got = [None] * members
        got[0] = parts[0]
        for s in partner_order(members):
            got[s] = lax.ppermute(parts[s], "chan", [(f, f ^ s) for f in range(members)])
        return got

    messages = exchange(messages)
    returned = call(
        functools.partial(owner_kernel, members, block, slots),
        [shape_of((2 * block, cols), WIRE)] * members, [vmem] * (1 + members), 16,
    )(rates, *messages)
    returned = exchange(returned)
    order = [0] + partner_order(members)
    early = len(order) * EARLY // 8
    outputs = []
    for group in (order[:early], order[early:]):
        spaces = [vmem] * (4 + len(group)) + [hbm] * len(outputs)
        outputs = call(
            functools.partial(finish_kernel, members, group),
            [shape_of((own_rows, cols))] * 2, spaces, 16,
            [
                vmem((len(group), block, cols), F32), vmem((len(group), block, cols), F32),
                pltpu.SemaphoreType.DMA((2, len(group))),
            ],
            {4 + len(group) + i: i for i in range(len(outputs))}, hbm,
        )(q, u, inverse, rates, *(returned[s] for s in group), *outputs)
    return outputs[0][None], outputs[1][None]


def solution(mesh):
    in_specs = (
        P(("obs", "chan"), "tm", None, None, None),
        P(("obs", "chan"), None, None),
        P("obs"),
        P("obs"),
        P(("obs", "chan"), None, None),
        P(("obs", "chan"), None, None),
    )
    out_specs = (P(("obs", "chan"), "tm", None), P(("obs", "chan"), "tm", None))
    return jax.shard_map(
        on_device, mesh=mesh, in_specs=in_specs, out_specs=out_specs, check_vma=False
    )
```

```python
import functools

import jax
import jax.numpy as jnp
import numpy as np
from jax import lax
from jax.experimental import pallas as pl
from jax.experimental.pallas import tpu as pltpu
from jax.sharding import PartitionSpec as P


POLY = 3
WIRE = jnp.bfloat16
F32 = jnp.float32
LANES = 128
TILE = 8
MIB = 1 << 20


def poly_basis(total_count):
    position = (2.0 * np.arange(total_count) + 1.0) / total_count - 1.0
    powers = np.stack([position**degree for degree in range(POLY)], axis=1)
    columns = []
    for degree in range(POLY):
        column = np.eye(POLY)[degree]
        for previous in columns:
            column = column - np.sum((powers @ column) * (powers @ previous)) * previous
        columns.append(column / np.sqrt(np.sum((powers @ column) ** 2)))
    return columns


def basis_at(channel, total_count):
    position = (2.0 * channel.astype(F32) + 1.0) * (1.0 / total_count) - 1.0
    values = []
    for column in poly_basis(total_count):
        value = jnp.float32(column[POLY - 1])
        for coefficient in column[POLY - 2 :: -1]:
            value = value * position + np.float32(coefficient)
        values.append(value)
    return values


def eye_mask(rows):
    shape = (rows, max(rows, LANES))
    return lax.broadcasted_iota(jnp.int32, shape, 0) == lax.broadcasted_iota(jnp.int32, shape, 1)


def twice(half):
    return jnp.concatenate([half, half], axis=1)


def fill_operands(xs_ref, slot, rounded, mask):
    half = rounded.shape[1] // 2
    masked = mask.astype(jnp.bfloat16) * rounded
    xs_ref[2 * slot] = masked
    xs_ref[2 * slot + 1] = jnp.concatenate([-masked[:, half:], masked[:, :half]], axis=1)


def gradient_rows(resid_ref, xs_ref, mask_ref, rows):
    total = None
    for t in range(resid_ref.shape[0]):
        product = jnp.dot(resid_ref[t, 0, rows, :], xs_ref[2 * t], preferred_element_type=F32)
        product += jnp.dot(resid_ref[t, 1, rows, :], xs_ref[2 * t + 1], preferred_element_type=F32)
        part = twice(mask_ref[t, rows, :]) * product
        total = part if total is None else total + part
    return total


def store_wide(message, first, block, value):
    for k in range(value.shape[1] // LANES):
        message[first + k * block : first + (k + 1) * block] = value[:, k * LANES : (k + 1) * LANES].astype(WIRE)


def half_start(index, rows):
    return pl.multiple_of(index * rows, rows)


def first_kernel(
    resid_hbm, flags_hbm, cluster_hbm, penalty_hbm, jones_hbm, duals_hbm,
    resid_ref, grad_ref, sent_ref, mask_ref, counts_ref, inverse_ref, rates_ref, duals_ref,
    flags_ref, cluster_ref, penalty_ref, jones_ref, xs_ref, sems,
):
    rows, cols = jones_ref.shape
    _, stations = flags_ref.shape
    share, own_rows = resid_ref.shape[0], duals_ref.shape[0]
    step = rows // PIECES
    cuts = [(sum(PARTS[:m]) * step, PARTS[m] * step) for m in range(len(PARTS))]
    own = pl.ds(half_start(lax.axis_index("tm"), own_rows), own_rows)
    small = [(flags_hbm, flags_ref), (cluster_hbm, cluster_ref), (penalty_hbm, penalty_ref)]
    pieces = small + [(jones_hbm, jones_ref), (duals_hbm.at[own, :], duals_ref)]
    for start, size in cuts:
        cut = pl.ds(start, size)
        pieces.append((resid_hbm.at[:, :, cut, :], resid_ref.at[:, :, cut, :]))
    copies = [pltpu.make_async_copy(src, dst, sems.at[k]) for k, (src, dst) in enumerate(pieces)]
    streams = copies[5:]
    for copy in copies[:3] + streams[:1] + copies[3:5] + streams[1:]:
        copy.start()

    for copy in copies[:3]:
        copy.wait()
    flags = flags_ref[...].astype(F32)
    pick = (
        lax.broadcasted_iota(jnp.int32, (rows, stations), 0) // 2
        == lax.broadcasted_iota(jnp.int32, (rows, stations), 1)
    ).astype(jnp.bfloat16)

    def rows_of(line):
        spread = jnp.broadcast_to(line, (LANES, stations)).astype(jnp.bfloat16)
        return lax.dot_general(pick, spread, (((1,), (1,)), ((), ())), preferred_element_type=F32)

    for t in range(share):
        line = flags_ref[pl.ds(lax.axis_index("tm") * share + t, 1), :].astype(F32)
        mask_ref[t] = rows_of(line)
    counts_ref[...] = rows_of(jnp.sum(flags, axis=0, keepdims=True))
    dirs = cluster_ref.shape[1]
    lane = lax.broadcasted_iota(jnp.int32, (dirs, cols), 1)
    spread = lax.rem(lane, cols // 2) // 2 == lax.broadcasted_iota(jnp.int32, (dirs, cols), 0)
    labels = jnp.broadcast_to(cluster_ref[...].astype(F32), (8, dirs)).astype(jnp.bfloat16)
    label = jnp.dot(labels, spread.astype(jnp.bfloat16), preferred_element_type=F32)
    rates = jnp.zeros((8, cols), F32)
    for k in range(penalty_ref.shape[1]):
        rates = jnp.where(label == k, penalty_ref[0:1, k : k + 1], rates)
    rates_ref[...] = rates

    copies[3].wait()
    rounded = jones_ref[...].astype(jnp.bfloat16)
    for t in range(share):
        fill_operands(xs_ref, t, rounded, twice(mask_ref[t]))
    for m, (start, size) in enumerate(cuts):
        cut = pl.ds(start, size)
        streams[m].wait()
        total = gradient_rows(resid_ref, xs_ref, mask_ref, cut)
        inverse_ref[cut, :] = 1.0 / (twice(counts_ref[cut, :]) + rates[0:1])
        if m == 0:
            copies[4].wait()
        half, offset = divmod(start, own_rows)
        mine = rates[0:1] * (lax.axis_index("tm") == half).astype(F32)
        total = total + mine * (jones_ref[cut, :] - duals_ref[offset : offset + size])
        grad_ref[cut, :] = total
        sent_ref[cut, :] = total.astype(WIRE)


def other_kernel(
    chunks, resid_ref, mine_ref, theirs_ref, mask_ref, inverse_ref, duals_ref,
    u_ref, other_ref, xs_ref,
):
    own_rows = u_ref.shape[0]
    jones = (mine_ref[...] + theirs_ref[...].astype(F32)) * inverse_ref[...]
    rounded = jones.astype(jnp.bfloat16)
    for t in range(resid_ref.shape[0]):
        fill_operands(xs_ref, t, rounded, twice(mask_ref[t]))
    own = pl.ds(half_start(lax.axis_index("tm"), own_rows), own_rows)
    u_ref[...] = (
        mine_ref[own, :] + theirs_ref[own, :].astype(F32)
    ) * inverse_ref[own, :] + duals_ref[...]
    step = own_rows // chunks
    for m in range(chunks):
        start = half_start(1 - lax.axis_index("tm"), own_rows) + m * step
        other_ref[m * step : (m + 1) * step] = gradient_rows(
            resid_ref, xs_ref, mask_ref, pl.ds(pl.multiple_of(start, step), step)
        ).astype(WIRE)


def own_kernel(
    chunks, members, resid_ref, xs_ref, mask_ref, u_ref, counts_ref, own_ref, *message_refs
):
    own_rows = own_ref.shape[0]
    step = own_rows // chunks
    base = half_start(lax.axis_index("tm"), own_rows)
    for m in range(chunks):
        own_ref[m * step : (m + 1) * step] = gradient_rows(
            resid_ref, xs_ref, mask_ref, pl.ds(pl.multiple_of(base + m * step, step), step)
        )
    block = own_rows // members
    eye = eye_mask(block)
    for s, message in enumerate(message_refs):
        offset = half_start(lax.axis_index("chan") ^ s, block)
        store_wide(message, 0, block, u_ref[pl.ds(offset, block), :])
        counts = counts_ref[pl.ds(pl.multiple_of(base + offset, block), block), :]
        line = jnp.sum(jnp.where(eye, counts, 0.0), axis=0, keepdims=True)
        first = 2 * block * (u_ref.shape[1] // LANES)
        message[first : first + TILE] = jnp.broadcast_to(line, (TILE, LANES)).astype(WIRE)


def pack_kernel(members, own_ref, theirs_ref, u_ref, inverse_ref, rates_ref, *refs):
    q_ref, message_refs = refs[members], refs[members + 1 :]
    own_rows = u_ref.shape[0]
    base = half_start(lax.axis_index("tm"), own_rows)
    block = own_rows // members
    rates = rates_ref[0:1]
    for s, message in enumerate(message_refs):
        offset = half_start(lax.axis_index("chan") ^ s, block)
        rows = pl.ds(offset, block)
        u = u_ref[rows, :]
        inverse = inverse_ref[pl.ds(pl.multiple_of(base + offset, block), block), :]
        q = (own_ref[rows, :] + theirs_ref[rows, :].astype(F32) - rates * u) * inverse
        q_ref[rows, :] = q
        store_wide(message, block * (u.shape[1] // LANES), block, u + q)


def self_share(weights):
    return sum(weight * weight for weight in weights[1:]) + weights[0] * weights[0]


def owner_kernel(members, block, slots, rates_ref, *refs):
    received, returned = refs[:members], refs[members:]
    rates, cols = rates_ref[0:1], rates_ref.shape[1]
    eye = eye_mask(block)
    table = [2.0 * rates / (float(count) + rates) for count in range(slots + 1)]
    weights = [basis_at(lax.axis_index("chan") ^ s, members) for s in range(members)]
    shares = [self_share(weight) for weight in weights]
    pieces = cols // LANES
    ends = 2 * block * pieces
    usable = []
    for s in range(members):
        line = received[s][ends : ends + TILE].astype(F32)[0:1]
        usable.append(jnp.sum(jnp.where(eye, line, 0.0), axis=1, keepdims=True))

    def combine(terms):
        total = terms[0]
        for term in terms[1:]:
            total = total + term
        return total

    for row in range(0, block, 2 * TILE):
        for k in range(pieces):
            lanes = slice(k * LANES, (k + 1) * LANES)
            here = slice(k * block + row, k * block + row + 2 * TILE)
            there = slice((pieces + k) * block + row, (pieces + k) * block + row + 2 * TILE)
            u = [received[s][here].astype(F32) for s in range(members)]
            coeffs = [combine([weights[s][p] * u[s] for s in range(members)]) for p in range(POLY)]
            w = [received[s][there].astype(F32) for s in range(members)]
            known = []
            for s in range(members):
                first = combine([weights[s][p] * coeffs[p] for p in range(POLY)])
                returned[s][row : row + 2 * TILE, lanes] = (first - shares[s] * u[s]).astype(WIRE)
                counts = usable[s][row : row + 2 * TILE]
                weight = table[0][:, lanes]
                for count in range(1, slots + 1):
                    weight = jnp.where(counts == count, table[count][:, lanes], weight)
                step = weight * first
                known.append(shares[s] * w[s] + step)
                w[s] = w[s] + step
            sums = [combine([weights[s][p] * w[s] for s in range(members)]) for p in range(POLY)]
            for s in range(members):
                second = combine([weights[s][p] * sums[p] for p in range(POLY)])
                returned[s][block + row : block + row + 2 * TILE, lanes] = (second - known[s]).astype(WIRE)


def finish_kernel(members, group, q_ref, u_ref, inverse_ref, rates_ref, *refs):
    received = refs[: len(group)]
    jones_hbm, duals_hbm, jones_ref, duals_ref, sems = refs[-5:]
    rates = 2.0 * rates_ref[0:1]
    share = self_share(basis_at(lax.axis_index("chan"), members))
    own_rows = u_ref.shape[0]
    block = own_rows // members
    base = half_start(lax.axis_index("tm"), own_rows)
    copies = []
    for k, s in enumerate(group):
        offset = half_start(lax.axis_index("chan") ^ s, block)
        rows = pl.ds(offset, block)
        inverse = inverse_ref[pl.ds(pl.multiple_of(base + offset, block), block), :]
        u, q = u_ref[rows, :], q_ref[rows, :]
        first = received[k][0:block].astype(F32) + share * u
        jones_ref[k] = q + rates * inverse * first
        duals_ref[k] = (1.0 - share) * (u + q) - received[k][block : 2 * block].astype(F32)
        for i, (src, dst) in enumerate(((jones_ref, jones_hbm), (duals_ref, duals_hbm))):
            copies.append(pltpu.make_async_copy(src.at[k], dst.at[rows, :], sems.at[i, k]))
            copies[-1].start()
    for copy in copies:
        copy.wait()


def shape_of(shape, dtype=F32):
    return jax.ShapeDtypeStruct(shape, dtype)


def in_vmem(shape, dtype=F32):
    return pltpu.VMEM(shape, dtype)


def call(kernel, outs, ins, limit, scratch=(), aliases={}, out_space=pltpu.VMEM):
    return pl.pallas_call(
        kernel, out_shape=tuple(outs), in_specs=[pl.BlockSpec(memory_space=space) for space in ins],
        out_specs=tuple(pl.BlockSpec(memory_space=out_space) for _ in outs), scratch_shapes=scratch,
        input_output_aliases=aliases,
        compiler_params=pltpu.CompilerParams(vmem_limit_bytes=limit * MIB),
    )


PIECES = 8
PARTS = (2, 2, 2, 2)
CHUNKS = 1
EARLY = 3


def partner_order(members):
    far = list(range(members - 1, members // 2 - 1, -1))
    near = list(range(members // 2 - 1, 0, -1))
    return far[:1] + [partner for pair in zip(far[1:], near) for partner in pair]


def on_device(residuals, flag_masks, cluster, penalty, jones_init, duals_init):
    members, halves = lax.axis_size("chan"), lax.axis_size("tm")
    share, rows = residuals.shape[1], residuals.shape[3]
    slots, cols = flag_masks.shape[1], jones_init.shape[2]
    own_rows = rows // halves
    block = own_rows // members
    vmem, hbm = pltpu.VMEM, pltpu.HBM
    bf16 = jnp.bfloat16

    resid, grad, sent, masks, counts, inverse, rates, duals0 = call(
        first_kernel,
        [
            in_vmem(residuals.shape[1:], bf16), in_vmem((rows, cols)), in_vmem((rows, cols), WIRE), in_vmem((share, rows, LANES)),
            in_vmem((rows, LANES)), in_vmem((rows, cols)), in_vmem((8, cols)), in_vmem((own_rows, cols)),
        ],
        [hbm] * 6, 40,
        [
            vmem((slots, rows // 2), jnp.int32), vmem((1, cluster.shape[0]), jnp.int32),
            vmem((1, penalty.shape[0]), F32), vmem((rows, cols), F32), vmem((2 * share, rows, cols), bf16),
            pltpu.SemaphoreType.DMA((5 + len(PARTS),)),
        ],
    )(*(
        pltpu.with_memory_space_constraint(x, hbm)
        for x in (residuals[0], flag_masks[0], cluster[None, :], penalty[None, :], jones_init[0], duals_init[0])
    ))

    swap = [(0, 1), (1, 0)]
    grad_other = lax.ppermute(sent, "tm", swap)
    u, other, xs = call(
        functools.partial(other_kernel, CHUNKS),
        [in_vmem((own_rows, cols)), in_vmem((own_rows, cols), WIRE), in_vmem((2 * share, rows, cols), bf16)],
        [vmem] * 6, 24,
    )(resid, grad, grad_other, masks, inverse, duals0)
    theirs = lax.ppermute(other, "tm", swap)
    message = in_vmem((2 * block * (cols // LANES) + TILE, LANES), WIRE)
    own, *messages = call(
        functools.partial(own_kernel, CHUNKS, members),
        [in_vmem((own_rows, cols))] + [message] * members, [vmem] * 5, 24,
    )(resid, xs, masks, u, counts)
    q, *messages = call(
        functools.partial(pack_kernel, members), [in_vmem((own_rows, cols))] + [message] * members,
        [vmem] * (5 + members), 16, aliases={5 + s: 1 + s for s in range(members)},
    )(own, theirs, u, inverse, rates, *messages)

    def exchange(parts):
        got = [None] * members
        got[0] = parts[0]
        for s in partner_order(members):
            got[s] = lax.ppermute(parts[s], "chan", [(f, f ^ s) for f in range(members)])
        return got

    messages = exchange(messages)
    returned = call(
        functools.partial(owner_kernel, members, block, slots),
        [shape_of((2 * block, cols), WIRE)] * members, [vmem] * (1 + members), 16,
    )(rates, *messages)
    returned = exchange(returned)
    order = [0] + partner_order(members)
    early = len(order) * EARLY // 8
    outputs = []
    for group in (order[:early], order[early:]):
        spaces = [vmem] * (4 + len(group)) + [hbm] * len(outputs)
        outputs = call(
            functools.partial(finish_kernel, members, group),
            [shape_of((own_rows, cols))] * 2, spaces, 16,
            [
                vmem((len(group), block, cols), F32), vmem((len(group), block, cols), F32),
                pltpu.SemaphoreType.DMA((2, len(group))),
            ],
            {4 + len(group) + i: i for i in range(len(outputs))}, hbm,
        )(q, u, inverse, rates, *(returned[s] for s in group), *outputs)
    return outputs[0][None], outputs[1][None]


def solution(mesh):
    in_specs = (
        P(("obs", "chan"), "tm", None, None, None),
        P(("obs", "chan"), None, None),
        P("obs"),
        P("obs"),
        P(("obs", "chan"), None, None),
        P(("obs", "chan"), None, None),
    )
    out_specs = (P(("obs", "chan"), "tm", None), P(("obs", "chan"), "tm", None))
    return jax.shard_map(
        on_device, mesh=mesh, in_specs=in_specs, out_specs=out_specs, check_vma=False
    )
```

```python
import functools

import jax
import jax.numpy as jnp
import numpy as np
from jax import lax
from jax.experimental import pallas as pl
from jax.experimental.pallas import tpu as pltpu
from jax.sharding import PartitionSpec as P


POLY = 3
WIRE = jnp.bfloat16
F32 = jnp.float32
LANES = 128
TILE = 8
MIB = 1 << 20


def poly_basis(total_count):
    position = (2.0 * np.arange(total_count) + 1.0) / total_count - 1.0
    powers = np.stack([position**degree for degree in range(POLY)], axis=1)
    columns = []
    for degree in range(POLY):
        column = np.eye(POLY)[degree]
        for previous in columns:
            column = column - np.sum((powers @ column) * (powers @ previous)) * previous
        columns.append(column / np.sqrt(np.sum((powers @ column) ** 2)))
    return columns


def basis_at(channel, total_count):
    position = (2.0 * channel.astype(F32) + 1.0) * (1.0 / total_count) - 1.0
    values = []
    for column in poly_basis(total_count):
        value = jnp.float32(column[POLY - 1])
        for coefficient in column[POLY - 2 :: -1]:
            value = value * position + np.float32(coefficient)
        values.append(value)
    return values


def eye_mask(rows):
    shape = (rows, max(rows, LANES))
    return lax.broadcasted_iota(jnp.int32, shape, 0) == lax.broadcasted_iota(jnp.int32, shape, 1)


def twice(half):
    return jnp.concatenate([half, half], axis=1)


def fill_operands(xs_ref, slot, rounded, mask):
    half = rounded.shape[1] // 2
    masked = mask.astype(jnp.bfloat16) * rounded
    xs_ref[2 * slot] = masked
    xs_ref[2 * slot + 1] = jnp.concatenate([-masked[:, half:], masked[:, :half]], axis=1)


def gradient_rows(resid_ref, xs_ref, mask_ref, rows):
    total = None
    for t in range(resid_ref.shape[0]):
        product = jnp.dot(resid_ref[t, 0, rows, :], xs_ref[2 * t], preferred_element_type=F32)
        product += jnp.dot(resid_ref[t, 1, rows, :], xs_ref[2 * t + 1], preferred_element_type=F32)
        part = twice(mask_ref[t, rows, :]) * product
        total = part if total is None else total + part
    return total


def store_wide(message, first, block, value):
    for k in range(value.shape[1] // LANES):
        message[first + k * block : first + (k + 1) * block] = value[:, k * LANES : (k + 1) * LANES].astype(WIRE)


def half_start(index, rows):
    return pl.multiple_of(index * rows, rows)


def first_kernel(
    resid_hbm, flags_hbm, cluster_hbm, penalty_hbm, jones_hbm, duals_hbm,
    resid_ref, grad_ref, sent_ref, mask_ref, counts_ref, inverse_ref, rates_ref, duals_ref,
    flags_ref, cluster_ref, penalty_ref, jones_ref, xs_ref, sems,
):
    rows, cols = jones_ref.shape
    _, stations = flags_ref.shape
    share, own_rows = resid_ref.shape[0], duals_ref.shape[0]
    step = rows // PIECES
    cuts = [(sum(PARTS[:m]) * step, PARTS[m] * step) for m in range(len(PARTS))]
    own = pl.ds(half_start(lax.axis_index("tm"), own_rows), own_rows)
    small = [(flags_hbm, flags_ref), (cluster_hbm, cluster_ref), (penalty_hbm, penalty_ref)]
    pieces = small + [(jones_hbm, jones_ref), (duals_hbm.at[own, :], duals_ref)]
    for start, size in cuts:
        cut = pl.ds(start, size)
        pieces.append((resid_hbm.at[:, :, cut, :], resid_ref.at[:, :, cut, :]))
    copies = [pltpu.make_async_copy(src, dst, sems.at[k]) for k, (src, dst) in enumerate(pieces)]
    streams = copies[5:]
    for copy in copies[:4] + streams[:1] + copies[4:5] + streams[1:]:
        copy.start()

    for copy in copies[:3]:
        copy.wait()
    flags = flags_ref[...].astype(F32)
    pick = (
        lax.broadcasted_iota(jnp.int32, (rows, stations), 0) // 2
        == lax.broadcasted_iota(jnp.int32, (rows, stations), 1)
    ).astype(jnp.bfloat16)

    def rows_of(line):
        spread = jnp.broadcast_to(line, (LANES, stations)).astype(jnp.bfloat16)
        return lax.dot_general(pick, spread, (((1,), (1,)), ((), ())), preferred_element_type=F32)

    for t in range(share):
        line = flags_ref[pl.ds(lax.axis_index("tm") * share + t, 1), :].astype(F32)
        mask_ref[t] = rows_of(line)
    counts_ref[...] = rows_of(jnp.sum(flags, axis=0, keepdims=True))
    dirs = cluster_ref.shape[1]
    lane = lax.broadcasted_iota(jnp.int32, (dirs, cols), 1)
    spread = lax.rem(lane, cols // 2) // 2 == lax.broadcasted_iota(jnp.int32, (dirs, cols), 0)
    labels = jnp.broadcast_to(cluster_ref[...].astype(F32), (8, dirs)).astype(jnp.bfloat16)
    label = jnp.dot(labels, spread.astype(jnp.bfloat16), preferred_element_type=F32)
    rates = jnp.zeros((8, cols), F32)
    for k in range(penalty_ref.shape[1]):
        rates = jnp.where(label == k, penalty_ref[0:1, k : k + 1], rates)
    rates_ref[...] = rates
    inverse_ref[...] = 1.0 / (twice(counts_ref[...]) + rates[0:1])

    copies[3].wait()
    rounded = jones_ref[...].astype(jnp.bfloat16)
    for t in range(share):
        fill_operands(xs_ref, t, rounded, twice(mask_ref[t]))
    for m, (start, size) in enumerate(cuts):
        cut = pl.ds(start, size)
        streams[m].wait()
        total = gradient_rows(resid_ref, xs_ref, mask_ref, cut)
        if m == 0:
            copies[4].wait()
        half, offset = divmod(start, own_rows)
        mine = rates[0:1] * (lax.axis_index("tm") == half).astype(F32)
        total = total + mine * (jones_ref[cut, :] - duals_ref[offset : offset + size])
        grad_ref[cut, :] = total
        sent_ref[cut, :] = total.astype(WIRE)


def other_kernel(
    chunks, resid_ref, mine_ref, theirs_ref, mask_ref, inverse_ref, duals_ref,
    u_ref, other_ref, xs_ref,
):
    own_rows = u_ref.shape[0]
    jones = (mine_ref[...] + theirs_ref[...].astype(F32)) * inverse_ref[...]
    rounded = jones.astype(jnp.bfloat16)
    for t in range(resid_ref.shape[0]):
        fill_operands(xs_ref, t, rounded, twice(mask_ref[t]))
    own = pl.ds(half_start(lax.axis_index("tm"), own_rows), own_rows)
    u_ref[...] = (
        mine_ref[own, :] + theirs_ref[own, :].astype(F32)
    ) * inverse_ref[own, :] + duals_ref[...]
    step = own_rows // chunks
    for m in range(chunks):
        start = half_start(1 - lax.axis_index("tm"), own_rows) + m * step
        other_ref[m * step : (m + 1) * step] = gradient_rows(
            resid_ref, xs_ref, mask_ref, pl.ds(pl.multiple_of(start, step), step)
        ).astype(WIRE)


def own_kernel(
    chunks, members, resid_ref, xs_ref, mask_ref, u_ref, counts_ref, own_ref, *message_refs
):
    own_rows = own_ref.shape[0]
    step = own_rows // chunks
    base = half_start(lax.axis_index("tm"), own_rows)
    for m in range(chunks):
        own_ref[m * step : (m + 1) * step] = gradient_rows(
            resid_ref, xs_ref, mask_ref, pl.ds(pl.multiple_of(base + m * step, step), step)
        )
    block = own_rows // members
    eye = eye_mask(block)
    for s, message in enumerate(message_refs):
        offset = half_start(lax.axis_index("chan") ^ s, block)
        store_wide(message, 0, block, u_ref[pl.ds(offset, block), :])
        counts = counts_ref[pl.ds(pl.multiple_of(base + offset, block), block), :]
        line = jnp.sum(jnp.where(eye, counts, 0.0), axis=0, keepdims=True)
        first = 2 * block * (u_ref.shape[1] // LANES)
        message[first : first + TILE] = jnp.broadcast_to(line, (TILE, LANES)).astype(WIRE)


def pack_kernel(members, own_ref, theirs_ref, u_ref, inverse_ref, rates_ref, *refs):
    q_ref, message_refs = refs[members], refs[members + 1 :]
    own_rows = u_ref.shape[0]
    base = half_start(lax.axis_index("tm"), own_rows)
    block = own_rows // members
    rates = rates_ref[0:1]
    for s, message in enumerate(message_refs):
        offset = half_start(lax.axis_index("chan") ^ s, block)
        rows = pl.ds(offset, block)
        u = u_ref[rows, :]
        inverse = inverse_ref[pl.ds(pl.multiple_of(base + offset, block), block), :]
        q = (own_ref[rows, :] + theirs_ref[rows, :].astype(F32) - rates * u) * inverse
        q_ref[rows, :] = q
        store_wide(message, block * (u.shape[1] // LANES), block, u + q)


def self_share(weights):
    return sum(weight * weight for weight in weights[1:]) + weights[0] * weights[0]


def owner_kernel(members, block, slots, rates_ref, *refs):
    received, returned = refs[:members], refs[members:]
    rates, cols = rates_ref[0:1], rates_ref.shape[1]
    eye = eye_mask(block)
    table = [2.0 * rates / (float(count) + rates) for count in range(slots + 1)]
    weights = [basis_at(lax.axis_index("chan") ^ s, members) for s in range(members)]
    shares = [self_share(weight) for weight in weights]
    pieces = cols // LANES
    ends = 2 * block * pieces
    usable = []
    for s in range(members):
        line = received[s][ends : ends + TILE].astype(F32)[0:1]
        usable.append(jnp.sum(jnp.where(eye, line, 0.0), axis=1, keepdims=True))

    def combine(terms):
        total = terms[0]
        for term in terms[1:]:
            total = total + term
        return total

    for row in range(0, block, 2 * TILE):
        for k in range(pieces):
            lanes = slice(k * LANES, (k + 1) * LANES)
            here = slice(k * block + row, k * block + row + 2 * TILE)
            there = slice((pieces + k) * block + row, (pieces + k) * block + row + 2 * TILE)
            u = [received[s][here].astype(F32) for s in range(members)]
            coeffs = [combine([weights[s][p] * u[s] for s in range(members)]) for p in range(POLY)]
            w = [received[s][there].astype(F32) for s in range(members)]
            known = []
            for s in range(members):
                first = combine([weights[s][p] * coeffs[p] for p in range(POLY)])
                returned[s][row : row + 2 * TILE, lanes] = (first - shares[s] * u[s]).astype(WIRE)
                counts = usable[s][row : row + 2 * TILE]
                weight = table[0][:, lanes]
                for count in range(1, slots + 1):
                    weight = jnp.where(counts == count, table[count][:, lanes], weight)
                step = weight * first
                known.append(shares[s] * w[s] + step)
                w[s] = w[s] + step
            sums = [combine([weights[s][p] * w[s] for s in range(members)]) for p in range(POLY)]
            for s in range(members):
                second = combine([weights[s][p] * sums[p] for p in range(POLY)])
                returned[s][block + row : block + row + 2 * TILE, lanes] = (second - known[s]).astype(WIRE)


def finish_kernel(members, group, q_ref, u_ref, inverse_ref, rates_ref, *refs):
    received = refs[: len(group)]
    jones_hbm, duals_hbm, jones_ref, duals_ref, sems = refs[-5:]
    rates = 2.0 * rates_ref[0:1]
    share = self_share(basis_at(lax.axis_index("chan"), members))
    own_rows = u_ref.shape[0]
    block = own_rows // members
    base = half_start(lax.axis_index("tm"), own_rows)
    copies = []
    for k, s in enumerate(group):
        offset = half_start(lax.axis_index("chan") ^ s, block)
        rows = pl.ds(offset, block)
        inverse = inverse_ref[pl.ds(pl.multiple_of(base + offset, block), block), :]
        u, q = u_ref[rows, :], q_ref[rows, :]
        first = received[k][0:block].astype(F32) + share * u
        jones_ref[k] = q + rates * inverse * first
        duals_ref[k] = (1.0 - share) * (u + q) - received[k][block : 2 * block].astype(F32)
        for i, (src, dst) in enumerate(((jones_ref, jones_hbm), (duals_ref, duals_hbm))):
            copies.append(pltpu.make_async_copy(src.at[k], dst.at[rows, :], sems.at[i, k]))
            copies[-1].start()
    for copy in copies:
        copy.wait()


def shape_of(shape, dtype=F32):
    return jax.ShapeDtypeStruct(shape, dtype)


def in_vmem(shape, dtype=F32):
    return pltpu.VMEM(shape, dtype)


def call(kernel, outs, ins, limit, scratch=(), aliases={}, out_space=pltpu.VMEM):
    return pl.pallas_call(
        kernel, out_shape=tuple(outs), in_specs=[pl.BlockSpec(memory_space=space) for space in ins],
        out_specs=tuple(pl.BlockSpec(memory_space=out_space) for _ in outs), scratch_shapes=scratch,
        input_output_aliases=aliases,
        compiler_params=pltpu.CompilerParams(vmem_limit_bytes=limit * MIB),
    )


PIECES = 8
PARTS = (2, 2, 2, 2)
CHUNKS = 1
EARLY = 5


def partner_order(members):
    far = list(range(members - 1, members // 2 - 1, -1))
    near = list(range(members // 2 - 1, 0, -1))
    return far[:1] + [partner for pair in zip(far[1:], near) for partner in pair]


def on_device(residuals, flag_masks, cluster, penalty, jones_init, duals_init):
    members, halves = lax.axis_size("chan"), lax.axis_size("tm")
    share, rows = residuals.shape[1], residuals.shape[3]
    slots, cols = flag_masks.shape[1], jones_init.shape[2]
    own_rows = rows // halves
    block = own_rows // members
    vmem, hbm = pltpu.VMEM, pltpu.HBM
    bf16 = jnp.bfloat16

    resid, grad, sent, masks, counts, inverse, rates, duals0 = call(
        first_kernel,
        [
            in_vmem(residuals.shape[1:], bf16), in_vmem((rows, cols)), in_vmem((rows, cols), WIRE), in_vmem((share, rows, LANES)),
            in_vmem((rows, LANES)), in_vmem((rows, cols)), in_vmem((8, cols)), in_vmem((own_rows, cols)),
        ],
        [hbm] * 6, 40,
        [
            vmem((slots, rows // 2), jnp.int32), vmem((1, cluster.shape[0]), jnp.int32),
            vmem((1, penalty.shape[0]), F32), vmem((rows, cols), F32), vmem((2 * share, rows, cols), bf16),
            pltpu.SemaphoreType.DMA((5 + len(PARTS),)),
        ],
    )(*(
        pltpu.with_memory_space_constraint(x, hbm)
        for x in (residuals[0], flag_masks[0], cluster[None, :], penalty[None, :], jones_init[0], duals_init[0])
    ))

    swap = [(0, 1), (1, 0)]
    grad_other = lax.ppermute(sent, "tm", swap)
    u, other, xs = call(
        functools.partial(other_kernel, CHUNKS),
        [in_vmem((own_rows, cols)), in_vmem((own_rows, cols), WIRE), in_vmem((2 * share, rows, cols), bf16)],
        [vmem] * 6, 24,
    )(resid, grad, grad_other, masks, inverse, duals0)
    theirs = lax.ppermute(other, "tm", swap)
    message = in_vmem((2 * block * (cols // LANES) + TILE, LANES), WIRE)
    own, *messages = call(
        functools.partial(own_kernel, CHUNKS, members),
        [in_vmem((own_rows, cols))] + [message] * members, [vmem] * 5, 24,
    )(resid, xs, masks, u, counts)
    q, *messages = call(
        functools.partial(pack_kernel, members), [in_vmem((own_rows, cols))] + [message] * members,
        [vmem] * (5 + members), 16, aliases={5 + s: 1 + s for s in range(members)},
    )(own, theirs, u, inverse, rates, *messages)

    def exchange(parts):
        got = [None] * members
        got[0] = parts[0]
        for s in partner_order(members):
            got[s] = lax.ppermute(parts[s], "chan", [(f, f ^ s) for f in range(members)])
        return got

    messages = exchange(messages)
    returned = call(
        functools.partial(owner_kernel, members, block, slots),
        [shape_of((2 * block, cols), WIRE)] * members, [vmem] * (1 + members), 16,
    )(rates, *messages)
    returned = exchange(returned)
    order = [0] + partner_order(members)
    early = len(order) * EARLY // 8
    outputs = []
    for group in (order[:early], order[early:]):
        spaces = [vmem] * (4 + len(group)) + [hbm] * len(outputs)
        outputs = call(
            functools.partial(finish_kernel, members, group),
            [shape_of((own_rows, cols))] * 2, spaces, 16,
            [
                vmem((len(group), block, cols), F32), vmem((len(group), block, cols), F32),
                pltpu.SemaphoreType.DMA((2, len(group))),
            ],
            {4 + len(group) + i: i for i in range(len(outputs))}, hbm,
        )(q, u, inverse, rates, *(returned[s] for s in group), *outputs)
    return outputs[0][None], outputs[1][None]


def solution(mesh):
    in_specs = (
        P(("obs", "chan"), "tm", None, None, None),
        P(("obs", "chan"), None, None),
        P("obs"),
        P("obs"),
        P(("obs", "chan"), None, None),
        P(("obs", "chan"), None, None),
    )
    out_specs = (P(("obs", "chan"), "tm", None), P(("obs", "chan"), "tm", None))
    return jax.shard_map(
        on_device, mesh=mesh, in_specs=in_specs, out_specs=out_specs, check_vma=False
    )
```
